256 devices in a mesh: wide: 64 (over z_hi, x, y, core), seq: 4 (over z_lo).
Axes of the slice: x: 4, y: 4, z: 8 (z_hi: 2, z_lo: 4; z = z_hi * 4 + z_lo), core: 2. Of those that a mesh axis runs over, the one named last changes fastest.
Arguments:
- features: bfloat16 [64, 128, 16, 384], P(None, 'wide', 'seq'), may hold values from -6 to 6
- clip_start: int32 [64], replicated, may hold values from 0 to 127, as said below
- clip_frames: int32 [64], replicated, may hold values from 1 to 128
- clip_group: int32 [64], replicated, may hold values from 0 to 63, each once
- conv_weight: bfloat16 [2, 3, 384, 384], replicated, may hold values from -0.1875 to 0.1875
- head_weight: bfloat16 [384, 16], replicated, may hold values from -0.3125 to 0.3125
- embed_weight: bfloat16 [64, 2560], replicated, may hold values from -0.75 to 0.75
- modulation_gain: float32 [2560], replicated, may hold values from 0.1 to 1.9
- modulation_shift: float32 [2560], replicated, may hold values from -3 to 3
- query_weight: bfloat16 [2560, 2560], P('wide', 'seq')
- key_weight: bfloat16 [2560, 2560], P('wide', 'seq')
- value_weight: bfloat16 [2560, 2560], P('wide', 'seq'), may hold values from -0.125 to 0.125
- query_gain: float32 [2560], P('seq')
- key_gain: float32 [2560], P('seq')
- read_weight: float32 [2560], P('seq'), may hold values from -1.2 to 1.2
Outputs:
- latent_grad: float32 [64, 128, 256], P('wide', None, 'seq')
The draws below stay inside these ranges and needn't reach their ends.
Inputs may be any that keep to these rules, and one draw needn't show every extreme that they name: Each clip occupies frame slots clip_start to clip_start + clip_frames - 1, and clip_start + clip_frames <= 128. `clip_group`: A permutation: every group holds exactly one clip.
All inputs are finite; a program needn't handle non-finite values.
Results may differ from the reference program's by a relative error of at most 0.029.
Values may be sent and summed in bfloat16 or wider, within the bound.
No kernel may reach another device: no remote copies, remote signals or barrier semaphores. Data moves between devices by JAX's collectives and lax.ppermute only.
A program may use at most 128 MiB of HBM per device.

```python
import math
import jax
import jax.numpy as jnp
from jax import lax

D = 2560
HEADS = 20
HDIM = 128
HW = 2560
C = 384
ZC = 16
P_SIZE = 64
KT = 3
LAYERS = 2
PIX = 16
CLIPS = 64
LMAX = 128
TOKENS = 512


def clip_layout(key):
    length_key = jax.random.fold_in(key, 101)
    full_key = jax.random.fold_in(key, 102)
    short_key = jax.random.fold_in(key, 103)
    start_key = jax.random.fold_in(key, 104)
    frames = jax.random.randint(length_key, (CLIPS,), 1, LMAX + 1, dtype=jnp.int32)
    full_clip = jax.random.randint(full_key, (), 0, CLIPS, dtype=jnp.int32)
    short_clip = (full_clip + 1 + jax.random.randint(short_key, (), 0, CLIPS - 1, dtype=jnp.int32)) % CLIPS
    indices = jnp.arange(CLIPS, dtype=jnp.int32)
    frames = jnp.where(indices == full_clip, LMAX, jnp.where(indices == short_clip, 1, frames)).astype(jnp.int32)
    starts = jax.random.randint(start_key, (CLIPS,), 0, LMAX - frames + 1, dtype=jnp.int32)
    starts = jnp.where(indices == short_clip, LMAX - 1, starts).astype(jnp.int32)
    return (starts, frames)


def draw_clip_start(key, part):
    return clip_layout(key)[0]


def draw_clip_frames(key, part):
    return clip_layout(key)[1]


def projection_pair(key):
    first_key = jax.random.fold_in(key, 201)
    second_key = jax.random.fold_in(key, 202)
    spread_scale = 1.0 / math.sqrt(D)
    query_side = jax.random.normal(first_key, (D, HW), jnp.float32) * spread_scale
    key_side = jax.random.normal(second_key, (D, HW), jnp.float32) * spread_scale
    return (query_side.astype(jnp.bfloat16), key_side.astype(jnp.bfloat16))


def draw_query_weight(key, part):
    return projection_pair(key)[0]


def draw_key_weight(key, part):
    return projection_pair(key)[1]


def gain_pair(key):
    query_key = jax.random.fold_in(key, 302)
    other_key = jax.random.fold_in(key, 303)
    query_side = jnp.exp(jax.random.uniform(query_key, (HEADS, HDIM), jnp.float32, -0.7, 0.7))
    key_side = jnp.exp(jax.random.uniform(other_key, (HEADS, HDIM), jnp.float32, -0.7, 0.7))
    return (query_side.reshape(HW), key_side.reshape(HW))


def draw_query_gain(key, part):
    return gain_pair(key)[0]


def draw_key_gain(key, part):
    return gain_pair(key)[1]


def block_scale(rng, shape, split, least, largest):
    factor_of = 1.0
    for position, parts in split:
        heights = jax.random.uniform(jax.random.fold_in(jax.random.fold_in(rng, 6), position), (parts,), jnp.float32, least / len(split), largest / len(split))
        factor_of = factor_of * jnp.repeat(jnp.exp(heights), shape[position] // parts).reshape((-1,) + (1,) * (len(shape) - 1 - position))
    return factor_of


def noise(rng, shape, width, most, pieces=(), held_as=jnp.bfloat16):
    drawn = width * jax.random.normal(rng, shape, jnp.float32)
    if pieces:
        drawn = drawn * block_scale(rng, shape, pieces, -0.22, 0.18)
    return jnp.clip(drawn, -most, most).astype(held_as)


def setup_inputs(seed: int = 0) -> dict:
    streams_of = jax.random.split(jax.random.key(seed), 16)
    return {
        "features": noise(streams_of[0], (CLIPS, LMAX, PIX, C), 1.0, 6.0, ((1, 64), (2, 4))),
        "clip_start": draw_clip_start(jax.random.fold_in(streams_of[15], 71), 0),
        "clip_frames": draw_clip_frames(jax.random.fold_in(streams_of[15], 71), 0),
        "clip_group": jax.random.permutation(streams_of[3], CLIPS).astype(jnp.int32),
        "conv_weight": noise(streams_of[4], (LAYERS, KT, C, C), (KT * C) ** -0.5, 0.1875),
        "head_weight": noise(streams_of[5], (C, ZC), C ** -0.5, 0.3125),
        "embed_weight": noise(streams_of[6], (P_SIZE, D), P_SIZE ** -0.5, 0.75),
        "modulation_gain": jnp.clip(1.0 + 0.18 * jax.random.normal(streams_of[7], (D,), jnp.float32), 0.1, 1.9),
        "modulation_shift": noise(streams_of[8], (D,), 0.5, 3.0, (), jnp.float32),
        "query_weight": draw_query_weight(jax.random.fold_in(streams_of[15], 71), 0),
        "key_weight": draw_key_weight(jax.random.fold_in(streams_of[15], 71), 0),
        "value_weight": noise(streams_of[11], (D, HW), D ** -0.5, 0.125, ((0, 64), (1, 4))),
        "query_gain": draw_query_gain(jax.random.fold_in(streams_of[15], 71), 0),
        "key_gain": draw_key_gain(jax.random.fold_in(streams_of[15], 71), 0),
        "read_weight": noise(streams_of[14], (HW,), 0.2, 1.2, ((0, 4),), jnp.float32),
    }


norm_eps = 1e-06

def normed_silu(values):
    widened = values.astype(jnp.float32)
    factor = lax.rsqrt(lax.optimization_barrier(jnp.mean(widened * widened, axis=-1, keepdims=True)) + norm_eps)
    return jax.nn.silu(widened * factor).astype(jnp.bfloat16)

def head_norm(projected, gains):
    factor = lax.rsqrt(lax.optimization_barrier(jnp.mean(projected * projected, axis=-1, keepdims=True)) + norm_eps)
    return ((projected * factor * gains).astype(jnp.bfloat16), factor)

def head_norm_back(projected, factor, gains, upstream):
    scaled = gains * upstream
    inner = lax.optimization_barrier(jnp.mean(projected * scaled, axis=-1, keepdims=True))
    return factor * scaled - projected * (factor * factor * factor) * inner

def critic_grad(tokens, token_valid, embed_weight, modulation_gain, modulation_shift, query_weight, key_weight, value_weight, query_gain, key_gain, read_weight):
    token_count = tokens.shape[0]
    hidden = jnp.dot(tokens, embed_weight, preferred_element_type=jnp.float32)
    center = lax.optimization_barrier(jnp.mean(hidden, axis=-1, keepdims=True))
    variance = lax.optimization_barrier(jnp.mean(jnp.square(hidden - center), axis=-1, keepdims=True))
    inverse = lax.rsqrt(variance + norm_eps)
    standard = (hidden - center) * inverse
    normed = (standard * modulation_gain + modulation_shift).astype(jnp.bfloat16)
    queries = jnp.dot(normed, query_weight, preferred_element_type=jnp.float32).reshape(token_count, HEADS, HDIM)
    keys_raw = jnp.dot(normed, key_weight, preferred_element_type=jnp.float32).reshape(token_count, HEADS, HDIM)
    values_b = jnp.dot(normed, value_weight, preferred_element_type=jnp.float32).astype(jnp.bfloat16).reshape(token_count, HEADS, HDIM)
    query_gains = query_gain.reshape(HEADS, HDIM)
    key_gains = key_gain.reshape(HEADS, HDIM)
    read_heads = read_weight.reshape(HEADS, HDIM)
    queries_n, query_factor = head_norm(queries, query_gains)
    keys_n, key_factor = head_norm(keys_raw, key_gains)
    root = jnp.sqrt(jnp.float32(HDIM))
    scores = jnp.einsum('ihd,jhd->hij', queries_n.astype(jnp.float32), keys_n.astype(jnp.float32)) / root
    scores = jnp.where(token_valid[None, None, :], scores, -jnp.inf)
    probs = jax.nn.softmax(scores, axis=-1)
    probs_b = probs.astype(jnp.bfloat16)
    query_mask = token_valid.astype(jnp.float32)
    readout = jnp.einsum('jhd,hd->hj', values_b.astype(jnp.float32), read_heads)
    column = jnp.einsum('hij,i->hj', probs_b.astype(jnp.float32), query_mask)
    value_grad = (jnp.transpose(column)[:, :, None] * read_heads[None]).astype(jnp.bfloat16)
    centered = readout[:, None, :] - lax.optimization_barrier(jnp.sum(probs * readout[:, None, :], axis=-1, keepdims=True))
    score_grad = (query_mask[None, :, None] * probs * centered).astype(jnp.bfloat16)
    query_back = jnp.einsum('hij,jhd->ihd', score_grad.astype(jnp.float32), keys_n.astype(jnp.float32)) / root
    key_back = jnp.einsum('hij,ihd->jhd', score_grad.astype(jnp.float32), queries_n.astype(jnp.float32)) / root
    query_grad = head_norm_back(queries, query_factor, query_gains, query_back).astype(jnp.bfloat16).reshape(token_count, HW)
    key_grad = head_norm_back(keys_raw, key_factor, key_gains, key_back).astype(jnp.bfloat16).reshape(token_count, HW)
    value_flat = value_grad.reshape(token_count, HW)
    normed_grad = jnp.dot(query_grad, jnp.transpose(query_weight), preferred_element_type=jnp.float32)
    normed_grad = normed_grad + jnp.dot(key_grad, jnp.transpose(key_weight), preferred_element_type=jnp.float32)
    normed_grad = normed_grad + jnp.dot(value_flat, jnp.transpose(value_weight), preferred_element_type=jnp.float32)
    scaled_grad = normed_grad * modulation_gain
    hidden_grad = inverse * (scaled_grad - lax.optimization_barrier(jnp.mean(scaled_grad, axis=-1, keepdims=True)) - standard * lax.optimization_barrier(jnp.mean(scaled_grad * standard, axis=-1, keepdims=True)))
    return jnp.dot(hidden_grad, jnp.transpose(embed_weight.astype(jnp.float32)), precision=lax.Precision.HIGHEST, preferred_element_type=jnp.float32)

def reference(features, clip_start, clip_frames, clip_group, conv_weight, head_weight, embed_weight, modulation_gain, modulation_shift, query_weight, key_weight, value_weight, query_gain, key_gain, read_weight):
    frame_ids = jnp.arange(LMAX, dtype=jnp.int32)
    clip_end = clip_start + clip_frames
    inside = (frame_ids[None, :] >= clip_start[:, None]) & (frame_ids[None, :] < clip_end[:, None])
    current = jnp.where(inside[:, :, None, None], features, jnp.zeros_like(features))
    margin = KT - 1
    for layer_index in range(LAYERS):
        active = normed_silu(current)
        padded = jnp.pad(active, ((0, 0), (margin, 0), (0, 0), (0, 0)))
        update = jnp.zeros(current.shape, jnp.float32)
        for tap_index in range(KT):
            offset = margin - tap_index
            update = update + jnp.einsum('cfpi,io->cfpo', padded[:, offset:offset + LMAX].astype(jnp.float32), conv_weight[layer_index, tap_index].astype(jnp.float32))
        current = (current.astype(jnp.float32) + update).astype(jnp.bfloat16)
    latent = jnp.einsum('cfpi,io->cfpo', normed_silu(current).astype(jnp.float32), head_weight.astype(jnp.float32))
    latent = jnp.where(inside[:, :, None, None], latent, jnp.zeros_like(latent)).astype(jnp.bfloat16)
    groups = jnp.arange(CLIPS, dtype=jnp.int32)
    holder = lax.optimization_barrier(jnp.sum(groups[None, :] * (clip_group[None, :] == groups[:, None]).astype(jnp.int32), axis=1)).astype(jnp.int32)

    def one_group(owner):
        tokens = latent[owner].reshape(TOKENS, P_SIZE)
        token_valid = jnp.repeat(inside[owner], PIX // 4)
        grads = critic_grad(tokens, token_valid, embed_weight, modulation_gain, modulation_shift, query_weight, key_weight, value_weight, query_gain, key_gain, read_weight)
        return grads.reshape(LMAX, PIX * ZC)
    return lax.map(one_group, holder)
```

```python
import functools

import jax
import jax.numpy as jnp
from jax import lax
from jax.experimental import pallas as pl
from jax.experimental.pallas import tpu as pltpu
from jax.sharding import PartitionSpec as P

HDIM = 128
norm_eps = 1e-06
F32 = jnp.float32
BF16 = jnp.bfloat16

GRID = (2, 4, 4, 2)
STRIDE = (32, 8, 2, 1)
FOLD_ROWS = 72
CHUNK_COLS = 384


def dot(a, b, contract=((1,), (0,))):
    return lax.dot_general(a, b, (contract, ((), ())), preferred_element_type=F32)


def split(values):
    high = values.astype(BF16)
    return high, (values - high.astype(F32)).astype(BF16)


def hop(block, place, distance):
    size, stride = GRID[place], STRIDE[place]
    route = []
    for source in range(64):
        here = source // stride % size
        there = (here + distance) % size
        route.append((source, source + (there - here) * stride))
    return lax.ppermute(block, "wide", route)


def pack_kernel(group_ref, feat_ref, wq_ref, wk_ref, wv_ref, embed_ref, gain_ref, shift_ref, out_ref, part_ref):
    wide = lax.axis_index("wide")
    rows = wq_ref.shape[0]
    width = wq_ref.shape[1]
    features = embed_ref.shape[1]
    base = wide * rows
    start = jnp.minimum(base // 128 * 128, features - 256)
    start = pl.multiple_of(start, 128)
    mean = jnp.mean(embed_ref[...].astype(F32), axis=1, keepdims=True)
    window = pl.ds(start, 256)
    scaled = (embed_ref[:, window].astype(F32) - mean) * gain_ref[:, window]
    joined = jnp.concatenate([scaled, shift_ref[:, window], jnp.zeros((7, 256), F32)], axis=0)
    joined = pltpu.roll(joined, lax.rem(256 - (base - start), 256), 1)[:, :rows]
    high, low = split(joined)
    for index, ref in enumerate((wq_ref, wk_ref, wv_ref)):
        weight = ref[...]
        part_ref[:, index * width : (index + 1) * width] = dot(high, weight) + dot(low, weight)
    columns = 3 * width // CHUNK_COLS
    for clip in range(group_ref.shape[0]):
        group = group_ref[clip]
        row = jnp.minimum(group // columns, FOLD_ROWS // 8 - 1) * 8
        column = lax.rem(group, columns) * CHUNK_COLS
        part = part_ref[pl.ds(pl.multiple_of(row, 8), 8), pl.ds(pl.multiple_of(column, 128), CHUNK_COLS)]
        frames = feat_ref[clip].astype(F32)
        slab = jnp.concatenate([frames[0], frames[1], part], axis=0)
        out_ref[group] = slab.astype(BF16)


def normed_silu(values):
    factor = lax.rsqrt(jnp.mean(values * values, axis=-1, keepdims=True) + norm_eps)
    scaled = values * factor
    return scaled * (1.0 / (1.0 + jnp.exp(-scaled)))


def own_span(group_ref, start_ref, frames_ref):
    wide = lax.axis_index("wide")
    clip = jnp.int32(0)
    for index in range(group_ref.shape[0]):
        clip = jnp.where(group_ref[index] == wide, jnp.int32(index), clip)
    first = start_ref[clip]
    return first, first + frames_ref[clip]


def encoder_kernel(group_ref, start_ref, frames_ref, slab_ref, conv_ref, head_ref, out_ref, spread_ref):
    first, last = own_span(group_ref, start_ref, frames_ref)
    channels = slab_ref.shape[2]
    slab = slab_ref[...].astype(F32)[:, :8, :]
    rows = slab.shape[0] * 8
    current = slab.reshape(rows, channels)
    row = lax.broadcasted_iota(jnp.int32, (rows, 1), 0)
    frame = row // 4
    current = jnp.where((frame >= first) & (frame < last), current, 0.0)
    for layer in range(conv_ref.shape[0]):
        active = normed_silu(current).astype(BF16)
        update = dot(active, conv_ref[layer, 0])
        for tap in range(1, conv_ref.shape[1]):
            behind = pltpu.roll(dot(active, conv_ref[layer, tap]), 4 * tap, 0)
            update = update + jnp.where(row >= 4 * tap, behind, 0.0)
        current = (current + update).astype(BF16).astype(F32)
    head = jnp.concatenate([head_ref[...]] * 8, axis=0)
    spread_ref[...] = dot(normed_silu(current).astype(BF16), head, ((1,), (1,)))
    frames = rows // 4
    lane = lax.broadcasted_iota(jnp.int32, (frames, 128), 1) // 16
    latent = jnp.zeros((frames, 128), F32)
    for position in range(4):
        latent = jnp.where(lane == position, spread_ref[pl.ds(position, frames, stride=4), :], latent)
    latent = latent[:, :64]
    own = lax.broadcasted_iota(jnp.int32, (frames, 1), 0)
    out_ref[...] = jnp.where((own >= first) & (own < last), latent, 0.0).astype(BF16)


def embed_kernel(t0_ref, t1_ref, t2_ref, t3_ref, embed_ref, inverse_ref, back_ref):
    embed = embed_ref[...]
    for index, ref in enumerate((t0_ref, t1_ref, t2_ref, t3_ref)):
        hidden = dot(ref[...], embed)
        hidden = hidden - jnp.mean(hidden, axis=1, keepdims=True)
        variance = jnp.mean(hidden * hidden, axis=1, keepdims=True)
        inverse_ref[index * 128 : (index + 1) * 128, :] = lax.rsqrt(variance + norm_eps)
        if index == 0:
            high, low = split(hidden)
            back_ref[...] = dot(high, embed, ((1,), (1,))) + dot(low, embed, ((1,), (1,)))


def critic_kernel(
    group_ref,
    start_ref,
    frames_ref,
    t0_ref,
    t1_ref,
    t2_ref,
    t3_ref,
    inverse_ref,
    near_ref,
    other_ref,
    qgain_ref,
    kgain_ref,
    read_ref,
    out_ref,
    fold_ref,
):
    first, last = own_span(group_ref, start_ref, frames_ref)
    wide = lax.axis_index("wide")
    place = [wide // STRIDE[i] % GRID[i] for i in range(4)]
    width = qgain_ref.shape[1]
    heads = width // HDIM
    columns = 3 * width // CHUNK_COLS
    for chunk in range(FOLD_ROWS // 8 * columns):
        away = [lax.rem(place[i] - chunk // STRIDE[i] % GRID[i] + GRID[i], GRID[i]) for i in range(4)]
        slot = (away[2] * 4 + away[1]) * 2 + away[0]
        values = jnp.where(away[3] == 0, near_ref[slot].astype(F32), other_ref[slot].astype(F32))
        row, column = chunk // columns * 8, chunk % columns * CHUNK_COLS
        fold_ref[row : row + 8, column : column + CHUNK_COLS] = values
    tokens = jnp.concatenate([t0_ref[...], t1_ref[...], t2_ref[...], t3_ref[...]], axis=0)
    rows = tokens.shape[0]
    inverse = inverse_ref[...]
    frames = rows // 4
    frame_down = lax.rem(lax.broadcasted_iota(jnp.int32, (rows, 1), 0), frames)
    frame_across = lax.rem(lax.broadcasted_iota(jnp.int32, (1, rows), 1), frames)
    key_bias = jnp.where((frame_down >= first) & (frame_down < last), 0.0, -jnp.inf)
    query_mask = jnp.where((frame_across >= first) & (frame_across < last), 1.0, 0.0)
    root = 1.0 / HDIM**0.5
    total = jnp.zeros((rows, 64), F32)
    for head in range(heads):
        spans = [pl.ds(part * width + head * HDIM, HDIM) for part in range(3)]
        here = pl.ds(head * HDIM, HDIM)
        folds = [fold_ref[:64, span].astype(BF16) for span in spans]
        q, k, v = (
            dot(tokens, fold) * inverse + fold_ref[64:65, span]
            for fold, span in zip(folds, spans, strict=True)
        )
        read = read_ref[:, here]
        qgain, kgain = qgain_ref[:, here], kgain_ref[:, here]
        rq = lax.rsqrt(jnp.mean(q * q, axis=1, keepdims=True) + norm_eps)
        rk = lax.rsqrt(jnp.mean(k * k, axis=1, keepdims=True) + norm_eps)
        qn = (q * rq * qgain).astype(BF16)
        kn = (k * rk * kgain).astype(BF16)
        readout = jnp.sum(v.astype(BF16).astype(F32) * read, axis=1, keepdims=True)
        scores = dot(kn, qn, ((1,), (1,))) + key_bias
        top = jnp.max(scores, axis=0, keepdims=True)
        weights = jnp.exp((scores - top) * root)
        probs = weights * (query_mask / jnp.sum(weights, axis=0, keepdims=True))
        column = jnp.sum(probs.astype(BF16).astype(F32), axis=1, keepdims=True)
        inner = jnp.sum(probs * readout, axis=0, keepdims=True)
        score_grad = (probs * (readout - inner)).astype(BF16)
        u = qgain * (dot(score_grad, kn, ((0,), (0,))) * root)
        w = kgain * (dot(score_grad, qn) * root)
        query_grad = rq * u - q * (rq * rq * rq) * jnp.mean(q * u, axis=1, keepdims=True)
        key_grad = rk * w - k * (rk * rk * rk) * jnp.mean(k * w, axis=1, keepdims=True)
        value_grad = column * read
        for grad, fold in zip((query_grad, key_grad, value_grad), folds, strict=True):
            total = total + dot(grad.astype(BF16), fold, ((1,), (1,)))
    out_ref[...] = total


def tail_kernel(features, own_ref, h1_ref, h2_ref, h3_ref, token_ref, inverse_ref, back_ref, out_ref):
    total = (own_ref[...] + h1_ref[...]) + (h2_ref[...] + h3_ref[...])
    inverse = inverse_ref[...]
    tokens = token_ref[...].astype(F32)
    inner = inverse * (jnp.sum(total * tokens, axis=1, keepdims=True) / features)
    out_ref[...] = (inverse * (total - (inner * inverse) * back_ref[...])).T


VMEM = pl.BlockSpec(memory_space=pltpu.VMEM)
SMEM = pl.BlockSpec(memory_space=pltpu.SMEM)


def call(kernel, scalars, arrays, out_shape, scratch=(), limit=48):
    return pl.pallas_call(
        kernel,
        in_specs=[SMEM] * len(scalars) + [VMEM] * len(arrays),
        out_specs=jax.tree.map(lambda _: VMEM, out_shape),
        out_shape=out_shape,
        scratch_shapes=list(scratch),
        compiler_params=pltpu.CompilerParams(vmem_limit_bytes=limit * 2**20),
    )(*scalars, *arrays)


def shape(dims, dtype):
    return jax.ShapeDtypeStruct(dims, dtype)


def on_device(
    features,
    clip_start,
    clip_frames,
    clip_group,
    conv_weight,
    head_weight,
    embed_weight,
    modulation_gain,
    modulation_shift,
    query_weight,
    key_weight,
    value_weight,
    query_gain,
    key_gain,
    read_weight,
):
    clips, channels = features.shape[0], features.shape[3]
    width = query_weight.shape[1]
    model = embed_weight.shape[1]
    with jax.named_scope("pack"):
        outgoing = call(
            pack_kernel,
            (clip_group,),
            (
                features,
                query_weight,
                key_weight,
                value_weight,
                embed_weight,
                modulation_gain[None],
                modulation_shift[None],
            ),
            shape((clips, 16, channels), BF16),
            (pltpu.VMEM((FOLD_ROWS, 3 * width), F32),),
        )
    with jax.named_scope("exchange"):
        slabs = lax.all_to_all(outgoing, "wide", split_axis=0, concat_axis=0, tiled=True)
    with jax.named_scope("fold"):
        mine = jnp.sum(slabs[:, 8:, :].astype(F32), axis=0).astype(BF16)[None]
        for place in (0, 1, 2):
            parts = [mine] + [hop(mine, place, d) for d in range(1, GRID[place])]
            mine = jnp.concatenate(parts, axis=0)
        other = hop(mine, 3, 1)
    spans = (clip_group, clip_start, clip_frames)
    with jax.named_scope("encoder"):
        tokens = call(
            encoder_kernel,
            spans,
            (slabs, conv_weight, head_weight.T),
            shape((128, 64), BF16),
            (pltpu.VMEM((512, 128), F32),),
        )
    with jax.named_scope("tokens"):
        blocks = [tokens] + [
            lax.ppermute(tokens, "seq", [(i, (i + d) % 4) for i in range(4)]) for d in (1, 2, 3)
        ]
        inverse, back = call(
            embed_kernel, (), (*blocks, embed_weight), (shape((512, 1), F32), shape((128, 64), F32))
        )
    with jax.named_scope("critic"):
        partial = call(
            critic_kernel,
            spans,
            (*blocks, inverse, mine, other, query_gain[None], key_gain[None], read_weight[None]),
            shape((512, 64), F32),
            (pltpu.VMEM((FOLD_ROWS, 3 * width), F32),),
        )
    with jax.named_scope("tail"):
        sums = [partial[:128]] + [
            lax.ppermute(partial[128 * d : 128 * (d + 1)], "seq", [(i, (i - d) % 4) for i in range(4)])
            for d in (1, 2, 3)
        ]
        result = call(
            functools.partial(tail_kernel, float(model)),
            (),
            (*sums, tokens, inverse[:128], back),
            shape((64, 128), F32),
        )
    return result.T[None]


def solution(mesh):
    return jax.shard_map(
        on_device,
        mesh=mesh,
        in_specs=(
            P(None, "wide", "seq", None),
            P(),
            P(),
            P(),
            P(),
            P(),
            P(),
            P(),
            P(),
            P("wide", "seq"),
            P("wide", "seq"),
            P("wide", "seq"),
            P("seq"),
            P("seq"),
            P("seq"),
        ),
        out_specs=P("wide", None, "seq"),
        check_vma=False,
    )
```

```python
import functools

import jax
import jax.numpy as jnp
from jax import lax
from jax.experimental import pallas as pl
from jax.experimental.pallas import tpu as pltpu
from jax.sharding import PartitionSpec as P

HDIM = 128
norm_eps = 1e-06
F32 = jnp.float32
BF16 = jnp.bfloat16

GRID = (2, 4, 4, 2)
STRIDE = (32, 8, 2, 1)
HALF = 32
HALVES = [list(range(HALF)), list(range(HALF, 2 * HALF))]
FOLD_ROWS = 72


def dot(a, b, contract=((1,), (0,))):
    return lax.dot_general(a, b, (contract, ((), ())), preferred_element_type=F32)


def split(values):
    high = values.astype(BF16)
    return high, (values - high.astype(F32)).astype(BF16)


def hop(block, place, distance):
    size, stride = GRID[place], STRIDE[place]
    route = []
    for source in range(64):
        here = source // stride % size
        there = (here + distance) % size
        route.append((source, source + (there - here) * stride))
    return lax.ppermute(block, "wide", route)


def pack_kernel(*refs):
    arrays, (out_ref, part_ref), held, sem, owner_ref = refs[:8], refs[8:10], refs[10:18], refs[18], refs[19]
    copies = [pltpu.make_async_copy(a, h, sem.at[i]) for i, (a, h) in enumerate(zip(arrays, held, strict=True))]
    for copy in copies:
        copy.start()
    feat_ref, *weights, embed_ref, gain_ref, shift_ref, group_ref = held
    wide = lax.axis_index("wide")
    rows, width = weights[0].shape
    features = embed_ref.shape[1]
    base = wide * rows
    start = jnp.minimum(base // 128 * 128, features - 256)
    start = pl.multiple_of(start, 128)
    for copy in copies[1:]:
        copy.wait()
    mean = jnp.mean(embed_ref[...].astype(F32), axis=1, keepdims=True)
    window = pl.ds(start, 256)
    scaled = (embed_ref[:, window].astype(F32) - mean) * gain_ref[window][None]
    joined = jnp.concatenate([scaled, shift_ref[window][None], jnp.zeros((7, 256), F32)], axis=0)
    joined = pltpu.roll(joined, lax.rem(256 - (base - start), 256), 1)[:, :rows]
    high, low = split(joined)
    for index, ref in enumerate(weights):
        weight = ref[...]
        part_ref[index] = dot(high, weight) + dot(low, weight)
    for clip in range(group_ref.shape[0]):
        owner_ref[group_ref[clip]] = jnp.int32(clip)
    copies[0].wait()
    channels = feat_ref.shape[3]
    for place in range(HALF):
        row = min(place // 3, FOLD_ROWS // 8 - 1) * 8
        part = part_ref[place % 3, row : row + 8, :]
        rest = jnp.concatenate([part[:, channels:], jnp.zeros((8, 2 * channels - width), F32)], axis=1)
        near = feat_ref[owner_ref[place]].astype(F32)
        far = feat_ref[owner_ref[HALF + place]].astype(F32)
        slab = jnp.concatenate([near[0], near[1], far[0], far[1], part[:, :channels], rest], axis=0)
        out_ref[place] = slab.astype(BF16)


def normed_silu(values):
    factor = lax.rsqrt(jnp.mean(values * values, axis=-1, keepdims=True) + norm_eps)
    scaled = values * factor
    return scaled * (1.0 / (1.0 + jnp.exp(-scaled)))


def span_of(group, group_ref, start_ref, frames_ref):
    clip = jnp.int32(0)
    for index in range(group_ref.shape[0]):
        clip = jnp.where(group_ref[index] == group, jnp.int32(index), clip)
    first = start_ref[clip]
    return first, first + frames_ref[clip]


def encoder_kernel(group_ref, start_ref, frames_ref, slab_ref, edge_ref, conv_ref, head_ref, keep_ref, send_ref, spread_ref):
    wide = lax.axis_index("wide")
    half, place = wide // HALF, lax.rem(wide, HALF)
    channels = slab_ref.shape[2]
    frames = slab_ref.shape[0] * 2
    ahead = edge_ref.shape[0] * 2
    rows = 4 * (frames + ahead)
    frame = frames * half - ahead + lax.broadcasted_iota(jnp.int32, (rows, 1), 0) // 4
    own = frames * half + lax.broadcasted_iota(jnp.int32, (frames, 1), 0)
    spans = [span_of(HALF * clip + place, group_ref, start_ref, frames_ref) for clip in range(2)]
    states = []
    for clip, (first, last) in enumerate(spans):
        here = slice(8 * clip, 8 * clip + 8)
        edge = edge_ref[...].astype(F32)[:, here].reshape(4 * ahead, channels)
        state = slab_ref[:, :16, :].astype(F32)[:, here].reshape(4 * frames, channels)
        state = jnp.concatenate([edge, state], axis=0)
        states.append(jnp.where((frame >= jnp.maximum(first, 0)) & (frame < last), state, 0.0))
    current = jnp.concatenate(states, axis=0)
    for layer in range(conv_ref.shape[0]):
        active = normed_silu(current).astype(BF16)
        update = dot(active, conv_ref[layer, 0])
        for tap in range(1, conv_ref.shape[1]):
            update = update + pltpu.roll(dot(active, conv_ref[layer, tap]), 4 * tap, 0)
        current = (current + update).astype(BF16).astype(F32)
    head = jnp.concatenate([head_ref[...]] * 8, axis=0)
    spread_ref[...] = dot(normed_silu(current).astype(BF16), head, ((1,), (1,)))
    lane = lax.broadcasted_iota(jnp.int32, (frames, 128), 1) // 16
    latents = []
    for clip, (first, last) in enumerate(spans):
        latent = jnp.zeros((frames, 128), F32)
        for position in range(4):
            values = spread_ref[pl.ds(rows * clip + 4 * ahead + position, frames, stride=4), :]
            latent = jnp.where(lane == position, values, latent)
        latents.append(jnp.where((own >= first) & (own < last), latent[:, :64], 0.0))
    keep_ref[...] = jnp.where(half == 0, latents[0], latents[1]).astype(BF16)
    send_ref[...] = jnp.where(half == 0, latents[1], latents[0]).astype(BF16)


def embed_kernel(t0_ref, t1_ref, t2_ref, t3_ref, embed_ref, inverse_ref, back_ref):
    embed = embed_ref[...]
    for index, ref in enumerate((t0_ref, t1_ref, t2_ref, t3_ref)):
        hidden = dot(ref[...], embed)
        hidden = hidden - jnp.mean(hidden, axis=1, keepdims=True)
        variance = jnp.mean(hidden * hidden, axis=1, keepdims=True)
        inverse_ref[index * 128 : (index + 1) * 128, :] = lax.rsqrt(variance + norm_eps)
        if index == 0:
            high, low = split(hidden)
            back_ref[...] = dot(high, embed, ((1,), (1,))) + dot(low, embed, ((1,), (1,)))


def critic_kernel(
    group_ref,
    start_ref,
    frames_ref,
    t0_ref,
    t1_ref,
    t2_ref,
    t3_ref,
    inverse_ref,
    near_ref,
    other_ref,
    qgain_ref,
    kgain_ref,
    read_ref,
    out_ref,
    fold_ref,
):
    wide = lax.axis_index("wide")
    first, last = span_of(wide, group_ref, start_ref, frames_ref)
    place = [wide // STRIDE[i] % GRID[i] for i in range(4)]
    width = qgain_ref.shape[1]
    heads = width // HDIM
    channels = near_ref.shape[2]
    for chunk in range(FOLD_ROWS // 8 * 3):
        away = [lax.rem(place[i] - chunk // STRIDE[i] % GRID[i] + GRID[i], GRID[i]) for i in range(4)]
        slot = away[2] * 4 + away[1]
        values = jnp.where(away[3] == 0, near_ref[slot].astype(F32), other_ref[slot].astype(F32))
        row, column = chunk // 3 * 8, chunk % 3 * width
        fold_ref[row : row + 8, column : column + channels] = values[:8]
        fold_ref[row : row + 8, column + channels : column + width] = values[8:, : width - channels]
    tokens = jnp.concatenate([t0_ref[...], t1_ref[...], t2_ref[...], t3_ref[...]], axis=0)
    rows = tokens.shape[0]
    inverse = inverse_ref[...]
    frames = rows // 4
    turn = place[0] * (frames // 2)
    frame_down = lax.rem(lax.broadcasted_iota(jnp.int32, (rows, 1), 0) + turn, frames)
    frame_across = lax.rem(lax.broadcasted_iota(jnp.int32, (1, rows), 1) + turn, frames)
    key_bias = jnp.where((frame_down >= first) & (frame_down < last), 0.0, -jnp.inf)
    query_mask = jnp.where((frame_across >= first) & (frame_across < last), 1.0, 0.0)
    root = 1.0 / HDIM**0.5
    total = jnp.zeros((rows, 64), F32)
    for head in range(heads):
        spans = [pl.ds(part * width + head * HDIM, HDIM) for part in range(3)]
        here = pl.ds(head * HDIM, HDIM)
        folds = [fold_ref[:64, span].astype(BF16) for span in spans]
        q, k, v = (
            dot(tokens, fold) * inverse + fold_ref[64:65, span]
            for fold, span in zip(folds, spans, strict=True)
        )
        read = read_ref[:, here]
        qgain, kgain = qgain_ref[:, here], kgain_ref[:, here]
        rq = lax.rsqrt(jnp.mean(q * q, axis=1, keepdims=True) + norm_eps)
        rk = lax.rsqrt(jnp.mean(k * k, axis=1, keepdims=True) + norm_eps)
        qn = (q * rq * qgain).astype(BF16)
        kn = (k * rk * kgain).astype(BF16)
        readout = jnp.sum(v.astype(BF16).astype(F32) * read, axis=1, keepdims=True)
        scores = dot(kn, qn, ((1,), (1,))) + key_bias
        top = jnp.max(scores, axis=0, keepdims=True)
        weights = jnp.exp((scores - top) * root)
        probs = weights * (query_mask / jnp.sum(weights, axis=0, keepdims=True))
        column = jnp.sum(probs.astype(BF16).astype(F32), axis=1, keepdims=True)
        inner = jnp.sum(probs * readout, axis=0, keepdims=True)
        score_grad = (probs * (readout - inner)).astype(BF16)
        u = qgain * (dot(score_grad, kn, ((0,), (0,))) * root)
        w = kgain * (dot(score_grad, qn) * root)
        query_grad = rq * u - q * (rq * rq * rq) * jnp.mean(q * u, axis=1, keepdims=True)
        key_grad = rk * w - k * (rk * rk * rk) * jnp.mean(k * w, axis=1, keepdims=True)
        value_grad = column * read
        for grad, fold in zip((query_grad, key_grad, value_grad), folds, strict=True):
            total = total + dot(grad.astype(BF16), fold, ((1,), (1,)))
    out_ref[...] = total


def tail_kernel(features, own_ref, h1_ref, h2_ref, h3_ref, token_ref, inverse_ref, back_ref, out_ref):
    total = (own_ref[...] + h1_ref[...]) + (h2_ref[...] + h3_ref[...])
    inverse = inverse_ref[...]
    tokens = token_ref[...].astype(F32)
    inner = inverse * (jnp.sum(total * tokens, axis=1, keepdims=True) / features)
    grad = inverse * (total - (inner * inverse) * back_ref[...])
    half = lax.axis_index("wide") // HALF
    frames = grad.shape[0]
    turned = jnp.concatenate([grad[frames // 2 :], grad[: frames // 2]], axis=0)
    out_ref[...] = jnp.where(half == 0, grad, turned).T


VMEM = pl.BlockSpec(memory_space=pltpu.VMEM)
SMEM = pl.BlockSpec(memory_space=pltpu.SMEM)


def call(kernel, scalars, arrays, out_shape, scratch=(), limit=48, space=VMEM):
    return pl.pallas_call(
        kernel,
        in_specs=[SMEM] * len(scalars) + [space] * len(arrays),
        out_specs=jax.tree.map(lambda _: VMEM, out_shape),
        out_shape=out_shape,
        scratch_shapes=list(scratch),
        compiler_params=pltpu.CompilerParams(vmem_limit_bytes=limit * 2**20),
    )(*scalars, *arrays)


def shape(dims, dtype):
    return jax.ShapeDtypeStruct(dims, dtype)


def on_device(
    features,
    clip_start,
    clip_frames,
    clip_group,
    conv_weight,
    head_weight,
    embed_weight,
    modulation_gain,
    modulation_shift,
    query_weight,
    key_weight,
    value_weight,
    query_gain,
    key_gain,
    read_weight,
):
    clips, channels = features.shape[0], features.shape[3]
    width = query_weight.shape[1]
    model = embed_weight.shape[1]
    with jax.named_scope("pack"):
        arrays = (
            features,
            query_weight,
            key_weight,
            value_weight,
            embed_weight,
            modulation_gain,
            modulation_shift,
            clip_group,
        )
        held = [pltpu.VMEM(a.shape, a.dtype) for a in arrays[:-1]] + [pltpu.SMEM((clips,), jnp.int32)]
        outgoing = call(
            pack_kernel,
            (),
            tuple(pltpu.with_memory_space_constraint(a, pltpu.HBM) for a in arrays),
            shape((HALF, 32, channels), BF16),
            (
                pltpu.VMEM((3, FOLD_ROWS, width), F32),
                *held,
                pltpu.SemaphoreType.DMA((len(arrays),)),
                pltpu.SMEM((clips,), jnp.int32),
            ),
            space=pl.BlockSpec(memory_space=pltpu.HBM),
        )
    with jax.named_scope("exchange"):
        slabs = lax.all_to_all(
            outgoing, "wide", split_axis=0, concat_axis=0, tiled=True, axis_index_groups=HALVES
        )
    spans = (clip_group, clip_start, clip_frames)

    def spread(piece, place):
        return jnp.concatenate([piece] + [hop(piece, place, d) for d in range(1, GRID[place])], axis=0)

    with jax.named_scope("halves"):
        half_sum = jnp.sum(slabs[:, 16:, :].astype(F32), axis=0).astype(BF16)[None]
        passed = hop(jnp.concatenate([half_sum, slabs[HALF - 2 :, :16]], axis=0), 0, 1)
        mine = (half_sum.astype(F32) + passed[:1].astype(F32)).astype(BF16)
        edge = passed[1:]
    with jax.named_scope("encoder"):
        keep, send = call(
            encoder_kernel,
            spans,
            (slabs, edge, conv_weight, head_weight.T),
            (shape((64, 64), BF16), shape((64, 64), BF16)),
            (pltpu.VMEM((544, 128), F32),),
        )
    mine, keep, send = lax.optimization_barrier((mine, keep, send))
    with jax.named_scope("tokens"):
        tokens = jnp.concatenate([keep, hop(send, 0, 1)], axis=0)
        blocks = [tokens] + [
            lax.ppermute(tokens, "seq", [(i, (i + d) % 4) for i in range(4)]) for d in (1, 2, 3)
        ]
        inverse, back = call(
            embed_kernel, (), (*blocks, embed_weight), (shape((512, 1), F32), shape((128, 64), F32))
        )
    with jax.named_scope("fold"):
        mine = spread(mine, 1)
        mine = spread(mine, 2)
        other = hop(mine, 3, 1)
    with jax.named_scope("critic"):
        partial = call(
            critic_kernel,
            spans,
            (*blocks, inverse, mine, other, query_gain[None], key_gain[None], read_weight[None]),
            shape((512, 64), F32),
            (pltpu.VMEM((FOLD_ROWS, 3 * width), F32),),
        )
    with jax.named_scope("tail"):
        sums = [partial[:128]] + [
            lax.ppermute(partial[128 * d : 128 * (d + 1)], "seq", [(i, (i - d) % 4) for i in range(4)])
            for d in (1, 2, 3)
        ]
        result = call(
            functools.partial(tail_kernel, float(model)),
            (),
            (*sums, blocks[0], inverse[:128], back),
            shape((64, 128), F32),
        )
    return result.T[None]


def solution(mesh):
    return jax.shard_map(
        on_device,
        mesh=mesh,
        in_specs=(
            P(None, "wide", "seq", None),
            P(),
            P(),
            P(),
            P(),
            P(),
            P(),
            P(),
            P(),
            P("wide", "seq"),
            P("wide", "seq"),
            P("wide", "seq"),
            P("seq"),
            P("seq"),
            P("seq"),
        ),
        out_specs=P("wide", None, "seq"),
        check_vma=False,
    )
```

```python
import functools

import jax
import jax.numpy as jnp
from jax import lax
from jax.experimental import pallas as pl
from jax.experimental.pallas import tpu as pltpu
from jax.sharding import PartitionSpec as P

HDIM = 128
norm_eps = 1e-06
LOG2E = 1.4426950408889634
F32 = jnp.float32
BF16 = jnp.bfloat16

HALF = 32
HALVES = [list(range(HALF)), list(range(HALF, 2 * HALF))]
FOLD_ROWS = 72


def dot(a, b, contract=((1,), (0,))):
    return lax.dot_general(a, b, (contract, ((), ())), preferred_element_type=F32)


def split(values):
    high = values.astype(BF16)
    return high, (values - high.astype(F32)).astype(BF16)


def swap(block, axis, bit):
    size = lax.axis_size(axis)
    return lax.ppermute(block, axis, [(place, place ^ bit) for place in range(size)])


def pack_kernel(*refs):
    arrays, (out_ref, part_ref), held, sem, owner_ref = refs[:8], refs[8:10], refs[10:18], refs[18], refs[19]
    copies = [pltpu.make_async_copy(a, h, sem.at[i]) for i, (a, h) in enumerate(zip(arrays, held, strict=True))]
    for copy in copies:
        copy.start()
    feat_ref, *weights, embed_ref, gain_ref, shift_ref, group_ref = held
    wide = lax.axis_index("wide")
    rows, width = weights[0].shape
    features = embed_ref.shape[1]
    base = wide * rows
    start = jnp.minimum(base // 128 * 128, features - 256)
    start = pl.multiple_of(start, 128)
    for copy in copies[1:]:
        copy.wait()
    mean = jnp.mean(embed_ref[...].astype(F32), axis=1, keepdims=True)
    window = pl.ds(start, 256)
    scaled = (embed_ref[:, window].astype(F32) - mean) * gain_ref[window][None]
    joined = jnp.concatenate([scaled, shift_ref[window][None], jnp.zeros((7, 256), F32)], axis=0)
    joined = pltpu.roll(joined, lax.rem(256 - (base - start), 256), 1)[:, :rows]
    high, low = split(joined)
    for index, ref in enumerate(weights):
        weight = ref[...]
        part_ref[index] = dot(high, weight) + dot(low, weight)
    for clip in range(group_ref.shape[0]):
        owner_ref[group_ref[clip]] = jnp.int32(clip)
    copies[0].wait()
    channels = feat_ref.shape[3]
    for place in range(HALF):
        row = min(place // 3, FOLD_ROWS // 8 - 1) * 8
        part = part_ref[place % 3, row : row + 8, :]
        rest = jnp.concatenate([part[:, channels:], jnp.zeros((8, 2 * channels - width), F32)], axis=1)
        near = feat_ref[owner_ref[place]].astype(F32)
        far = feat_ref[owner_ref[HALF + place]].astype(F32)
        slab = jnp.concatenate([near[0], near[1], far[0], far[1], part[:, :channels], rest], axis=0)
        out_ref[place] = slab.astype(BF16)


def normed_silu(values):
    factor = lax.rsqrt(jnp.mean(values * values, axis=-1, keepdims=True) + norm_eps)
    scaled = values * factor
    return scaled * (1.0 / (1.0 + jnp.exp(-scaled)))


def span_of(group, group_ref, start_ref, frames_ref):
    clip = jnp.int32(0)
    for index in range(group_ref.shape[0]):
        clip = jnp.where(group_ref[index] == group, jnp.int32(index), clip)
    first = start_ref[clip]
    return first, first + frames_ref[clip]


def encoder_kernel(group_ref, start_ref, frames_ref, slab_ref, edge_ref, conv_ref, head_ref, embed_ref, keep_ref, send_ref, spread_ref):
    wide = lax.axis_index("wide")
    half, place = wide // HALF, lax.rem(wide, HALF)
    channels = slab_ref.shape[2]
    frames = slab_ref.shape[0] * 2
    ahead = edge_ref.shape[0] * 2
    rows = 4 * (frames + ahead)
    frame = frames * half - ahead + lax.broadcasted_iota(jnp.int32, (rows, 1), 0) // 4
    own = frames * half + lax.broadcasted_iota(jnp.int32, (frames, 1), 0)
    spans = [span_of(HALF * clip + place, group_ref, start_ref, frames_ref) for clip in range(2)]
    states = []
    for clip, (first, last) in enumerate(spans):
        here = slice(8 * clip, 8 * clip + 8)
        edge = edge_ref[...].astype(F32)[:, here].reshape(4 * ahead, channels)
        state = slab_ref[:, :16, :].astype(F32)[:, here].reshape(4 * frames, channels)
        state = jnp.concatenate([edge, state], axis=0)
        states.append(jnp.where((frame >= jnp.maximum(first, 0)) & (frame < last), state, 0.0))
    current = jnp.concatenate(states, axis=0)
    for layer in range(conv_ref.shape[0]):
        active = normed_silu(current).astype(BF16)
        update = dot(active, conv_ref[layer, 0])
        for tap in range(1, conv_ref.shape[1]):
            update = update + pltpu.roll(dot(active, conv_ref[layer, tap]), 4 * tap, 0)
        current = (current + update).astype(BF16).astype(F32)
    head = jnp.concatenate([head_ref[...]] * 8, axis=0)
    spread_ref[...] = dot(normed_silu(current).astype(BF16), head, ((1,), (1,)))
    lane = lax.broadcasted_iota(jnp.int32, (frames, 128), 1) // 16
    latents = []
    for clip, (first, last) in enumerate(spans):
        latent = jnp.zeros((frames, 128), F32)
        for position in range(4):
            values = spread_ref[pl.ds(rows * clip + 4 * ahead + position, frames, stride=4), :]
            latent = jnp.where(lane == position, values, latent)
        latents.append(jnp.where((own >= first) & (own < last), latent, 0.0))
    tokens = jnp.concatenate(latents, axis=0).astype(BF16)
    hidden = dot(tokens[:, :64], embed_ref[...])
    hidden = hidden - jnp.mean(hidden, axis=1, keepdims=True)
    inverse = lax.rsqrt(jnp.mean(hidden * hidden, axis=1, keepdims=True) + norm_eps)
    lane = lax.broadcasted_iota(jnp.int32, tokens.shape, 1)
    packed = tokens.astype(F32)
    for term in range(3):
        high = inverse.astype(BF16).astype(F32)
        packed = jnp.where(lane == 64 + term, high, packed)
        inverse = inverse - high
    keep_ref[...] = jnp.where(half == 0, packed[:frames], packed[frames:]).astype(BF16)
    send_ref[...] = jnp.where(half == 0, packed[frames:], packed[:frames]).astype(BF16)


def back_kernel(token_ref, embed_ref, out_ref):
    embed = embed_ref[...]
    hidden = dot(token_ref[:, :64], embed)
    high, low = split(hidden - jnp.mean(hidden, axis=1, keepdims=True))
    out_ref[...] = dot(embed, high, ((1,), (1,))) + dot(embed, low, ((1,), (1,)))


def critic_kernel(
    group_ref,
    start_ref,
    frames_ref,
    t0_ref,
    t1_ref,
    t2_ref,
    t3_ref,
    near_ref,
    other_ref,
    qgain_ref,
    kgain_ref,
    read_ref,
    *refs,
):
    out_refs, fold_ref = refs[:4], refs[4]
    wide = lax.axis_index("wide")
    first, last = span_of(wide, group_ref, start_ref, frames_ref)
    half, place = wide // HALF, lax.rem(wide, HALF)
    width = qgain_ref.shape[1]
    heads = width // HDIM
    channels = near_ref.shape[2]
    for chunk in range(FOLD_ROWS // 8 * 3):
        apart = [lax.rem(place // bit + chunk // bit, 2) for bit in (8, 16, 2, 4, 1)]
        slot = sum(differs * 2**step for step, differs in enumerate(apart[:4]))
        values = jnp.where(apart[4] == 0, near_ref[slot].astype(F32), other_ref[slot].astype(F32))
        row, column = chunk // 3 * 8, chunk % 3 * width
        fold_ref[row : row + 8, column : column + channels] = values[:8]
        fold_ref[row : row + 8, column + channels : column + width] = values[8:, : width - channels]
    blocks = jnp.concatenate([t0_ref[...], t1_ref[...], t2_ref[...], t3_ref[...]], axis=0)
    tokens = blocks[:, :64]
    rows = tokens.shape[0]
    term = lax.broadcasted_iota(jnp.int32, (128, HDIM), 0)
    inverse = dot(blocks, jnp.where((term >= 64) & (term < 67), 1.0, 0.0).astype(BF16))
    frames = rows // 4
    turn = half * (frames // 2)
    frame_down = lax.rem(lax.broadcasted_iota(jnp.int32, (rows, 1), 0) + turn, frames)
    frame_across = lax.rem(lax.broadcasted_iota(jnp.int32, (1, rows), 1) + turn, frames)
    key_bias = jnp.where((frame_down >= first) & (frame_down < last), 0.0, -jnp.inf)
    query_mask = jnp.where((frame_across >= first) & (frame_across < last), 1.0, 0.0)
    root = 1.0 / HDIM**0.5
    total = jnp.zeros((rows, 64), F32)
    for head in range(heads):
        spans = [pl.ds(part * width + head * HDIM, HDIM) for part in range(3)]
        here = pl.ds(head * HDIM, HDIM)
        folds = [fold_ref[:64, span].astype(BF16) for span in spans]
        q, k, v = (
            dot(tokens, fold) * inverse + fold_ref[64:65, span]
            for fold, span in zip(folds, spans, strict=True)
        )
        read = read_ref[:, here]
        qgain, kgain = qgain_ref[:, here], kgain_ref[:, here]
        rq = lax.rsqrt(jnp.mean(q * q, axis=1, keepdims=True) + norm_eps)
        rk = lax.rsqrt(jnp.mean(k * k, axis=1, keepdims=True) + norm_eps)
        qn = (q * rq * qgain).astype(BF16)
        kn = (k * rk * kgain).astype(BF16)
        readout = jnp.sum(v.astype(BF16).astype(F32) * read, axis=1, keepdims=True)
        scores = dot(kn, qn, ((1,), (1,))) + key_bias
        top = jnp.max(scores, axis=0, keepdims=True)
        weights = jnp.exp2((scores - top) * (root * LOG2E))
        share = query_mask / jnp.sum(weights, axis=0, keepdims=True)
        inner = share * jnp.sum(weights * readout, axis=0, keepdims=True)
        probs = weights * share
        column = jnp.sum(probs, axis=1, keepdims=True)
        score_grad = (probs * (readout - inner)).astype(BF16)
        u = qgain * (dot(score_grad, kn, ((0,), (0,))) * root)
        w = kgain * (dot(score_grad, qn) * root)
        query_grad = rq * u - q * (rq * rq * rq) * jnp.mean(q * u, axis=1, keepdims=True)
        key_grad = rk * w - k * (rk * rk * rk) * jnp.mean(k * w, axis=1, keepdims=True)
        value_grad = column * read
        for grad, fold in zip((query_grad, key_grad, value_grad), folds, strict=True):
            total = total + dot(grad.astype(BF16), fold, ((1,), (1,)))
    for index, ref in enumerate(out_refs):
        ref[...] = total[index * frames : (index + 1) * frames]


def tail_kernel(features, own_ref, h1_ref, h2_ref, h3_ref, token_ref, back_ref, out_ref):
    total = ((own_ref[...] + h1_ref[...]) + (h2_ref[...] + h3_ref[...])).T
    turned = token_ref[...].astype(F32).T
    inverse = turned[64:65] + turned[65:66] + turned[66:67]
    inner = inverse * (jnp.sum(total * turned[:64], axis=0, keepdims=True) / features)
    grad = inverse * (total - (inner * inverse) * back_ref[...])
    half = lax.axis_index("wide") // HALF
    frames = grad.shape[1]
    out_ref[...] = jnp.where(half == 0, grad, pltpu.roll(grad, frames // 2, 1))


VMEM = pl.BlockSpec(memory_space=pltpu.VMEM)
SMEM = pl.BlockSpec(memory_space=pltpu.SMEM)


def call(kernel, scalars, arrays, out_shape, scratch=(), limit=48, space=VMEM):
    return pl.pallas_call(
        kernel,
        in_specs=[SMEM] * len(scalars) + [space] * len(arrays),
        out_specs=jax.tree.map(lambda _: VMEM, out_shape),
        out_shape=out_shape,
        scratch_shapes=list(scratch),
        compiler_params=pltpu.CompilerParams(vmem_limit_bytes=limit * 2**20),
    )(*scalars, *arrays)


def shape(dims, dtype):
    return jax.ShapeDtypeStruct(dims, dtype)


def on_device(
    features,
    clip_start,
    clip_frames,
    clip_group,
    conv_weight,
    head_weight,
    embed_weight,
    modulation_gain,
    modulation_shift,
    query_weight,
    key_weight,
    value_weight,
    query_gain,
    key_gain,
    read_weight,
):
    clips, channels = features.shape[0], features.shape[3]
    width = query_weight.shape[1]
    model = embed_weight.shape[1]
    with jax.named_scope("pack"):
        arrays = (
            features,
            query_weight,
            key_weight,
            value_weight,
            embed_weight,
            modulation_gain,
            modulation_shift,
            clip_group,
        )
        held = [pltpu.VMEM(a.shape, a.dtype) for a in arrays[:-1]] + [pltpu.SMEM((clips,), jnp.int32)]
        outgoing = call(
            pack_kernel,
            (),
            tuple(pltpu.with_memory_space_constraint(a, pltpu.HBM) for a in arrays),
            shape((HALF, 32, channels), BF16),
            (
                pltpu.VMEM((3, FOLD_ROWS, width), F32),
                *held,
                pltpu.SemaphoreType.DMA((len(arrays),)),
                pltpu.SMEM((clips,), jnp.int32),
            ),
            space=pl.BlockSpec(memory_space=pltpu.HBM),
        )
    with jax.named_scope("exchange"):
        slabs = lax.all_to_all(
            outgoing, "wide", split_axis=0, concat_axis=0, tiled=True, axis_index_groups=HALVES
        )
    spans = (clip_group, clip_start, clip_frames)

    def joined(piece, axis, low):
        return [piece] + [swap(piece, axis, low * apart) for apart in (1, 2, 3)]

    with jax.named_scope("halves"):
        half_sum = jnp.sum(slabs[:, 16:, :].astype(F32), axis=0).astype(BF16)[None]
        passed = swap(jnp.concatenate([half_sum, slabs[HALF - 2 :, :16]], axis=0), "wide", HALF)
        mine = (half_sum.astype(F32) + passed[:1].astype(F32)).astype(BF16)
        edge = passed[1:]
    with jax.named_scope("encoder"):
        keep, send = call(
            encoder_kernel,
            spans,
            (slabs, edge, conv_weight, head_weight.T, embed_weight),
            (shape((64, 128), BF16), shape((64, 128), BF16)),
            (pltpu.VMEM((544, 128), F32),),
        )
    with jax.named_scope("rounds"):
        mine = jnp.concatenate(joined(mine, "wide", 8), axis=0)
        mine, keep, send = lax.optimization_barrier((mine, keep, send))
        tokens = jnp.concatenate([keep, swap(send, "wide", HALF)], axis=0)
        mine = jnp.concatenate(joined(mine, "wide", 2), axis=0)
        mine, tokens = lax.optimization_barrier((mine, tokens))
        other = swap(mine, "wide", 1)
        blocks = joined(tokens, "seq", 1)
    with jax.named_scope("critic"):
        sums = call(
            critic_kernel,
            spans,
            (*blocks, mine, other, query_gain[None], key_gain[None], read_weight[None]),
            (shape((128, 64), F32),) * 4,
            (pltpu.VMEM((FOLD_ROWS, 3 * width), F32),),
        )
    with jax.named_scope("tail"):
        *sums, own = lax.optimization_barrier((*sums, blocks[0]))
        back = call(back_kernel, (), (own, embed_weight), shape((64, 128), F32))
        result = call(
            functools.partial(tail_kernel, float(model)),
            (),
            (sums[0], *(swap(sums[d], "seq", d) for d in (1, 2, 3)), own, back),
            shape((64, 128), F32),
        )
    return result.T[None]


def solution(mesh):
    return jax.shard_map(
        on_device,
        mesh=mesh,
        in_specs=(
            P(None, "wide", "seq", None),
            P(),
            P(),
            P(),
            P(),
            P(),
            P(),
            P(),
            P(),
            P("wide", "seq"),
            P("wide", "seq"),
            P("wide", "seq"),
            P("seq"),
            P("seq"),
            P("seq"),
        ),
        out_specs=P("wide", None, "seq"),
        check_vma=False,
    )
```

```python
import functools

import jax
import jax.numpy as jnp
from jax import lax
from jax.experimental import pallas as pl
from jax.experimental.pallas import tpu as pltpu
from jax.sharding import PartitionSpec as P

HDIM = 128
norm_eps = 1e-06
LOG2E = 1.4426950408889634
F32 = jnp.float32
BF16 = jnp.bfloat16

HALF = 32
HALVES = [list(range(HALF)), list(range(HALF, 2 * HALF))]
FOLD_ROWS = 72


def dot(a, b, contract=((1,), (0,))):
    return lax.dot_general(a, b, (contract, ((), ())), preferred_element_type=F32)


def split(values):
    high = values.astype(BF16)
    return high, (values - high.astype(F32)).astype(BF16)


def swap(block, axis, bit):
    size = lax.axis_size(axis)
    return lax.ppermute(block, axis, [(place, place ^ bit) for place in range(size)])


def pack_kernel(*refs):
    arrays, (out_ref, part_ref), held, sem, owner_ref = refs[:8], refs[8:10], refs[10:18], refs[18], refs[19]
    copies = [pltpu.make_async_copy(a, h, sem.at[i]) for i, (a, h) in enumerate(zip(arrays, held, strict=True))]
    for copy in copies:
        copy.start()
    feat_ref, *weights, embed_ref, gain_ref, shift_ref, group_ref = held
    wide = lax.axis_index("wide")
    rows, width = weights[0].shape
    features = embed_ref.shape[1]
    base = wide * rows
    start = jnp.minimum(base // 128 * 128, features - 256)
    start = pl.multiple_of(start, 128)
    for copy in copies[1:]:
        copy.wait()
    mean = jnp.mean(embed_ref[...].astype(F32), axis=1, keepdims=True)
    window = pl.ds(start, 256)
    scaled = (embed_ref[:, window].astype(F32) - mean) * gain_ref[window][None]
    joined = jnp.concatenate([scaled, shift_ref[window][None], jnp.zeros((7, 256), F32)], axis=0)
    joined = pltpu.roll(joined, lax.rem(256 - (base - start), 256), 1)[:, :rows]
    high, low = split(joined)
    for index, ref in enumerate(weights):
        weight = ref[...]
        part_ref[index] = dot(high, weight) + dot(low, weight)
    for clip in range(group_ref.shape[0]):
        owner_ref[group_ref[clip]] = jnp.int32(clip)
    copies[0].wait()
    channels = feat_ref.shape[3]
    for place in range(HALF):
        row = min(place // 3, FOLD_ROWS // 8 - 1) * 8
        part = part_ref[place % 3, row : row + 8, :]
        rest = jnp.concatenate([part[:, channels:], jnp.zeros((8, 2 * channels - width), F32)], axis=1)
        near = feat_ref[owner_ref[place]].astype(F32)
        far = feat_ref[owner_ref[HALF + place]].astype(F32)
        slab = jnp.concatenate([near[0], near[1], far[0], far[1], part[:, :channels], rest], axis=0)
        out_ref[place] = slab.astype(BF16)


def normed_silu(values):
    factor = lax.rsqrt(jnp.mean(values * values, axis=-1, keepdims=True) + norm_eps)
    scaled = values * factor
    return scaled * (1.0 / (1.0 + jnp.exp(-scaled)))


def span_of(group, group_ref, start_ref, frames_ref):
    clip = jnp.int32(0)
    for index in range(group_ref.shape[0]):
        clip = jnp.where(group_ref[index] == group, jnp.int32(index), clip)
    first = start_ref[clip]
    return first, first + frames_ref[clip]


def encode(slab, edge, spans, half, start, conv_ref, head_ref, embed_ref, spread_ref):
    channels = slab.shape[2]
    frames = slab.shape[0] * 2
    ahead = edge.shape[0] * 2
    rows = 4 * (frames + ahead)
    frame = start - ahead + lax.broadcasted_iota(jnp.int32, (rows, 1), 0) // 4
    own = start + lax.broadcasted_iota(jnp.int32, (frames, 1), 0)
    states = []
    for clip, (first, last) in enumerate(spans):
        here = slice(8 * clip, 8 * clip + 8)
        state = jnp.concatenate(
            [edge[:, here].reshape(4 * ahead, channels), slab[:, here].reshape(4 * frames, channels)], axis=0
        )
        states.append(jnp.where((frame >= jnp.maximum(first, 0)) & (frame < last), state, 0.0))
    current = jnp.concatenate(states, axis=0)
    for layer in range(conv_ref.shape[0]):
        active = normed_silu(current).astype(BF16)
        update = dot(active, conv_ref[layer, 0])
        for tap in range(1, conv_ref.shape[1]):
            update = update + pltpu.roll(dot(active, conv_ref[layer, tap]), 4 * tap, 0)
        current = (current + update).astype(BF16).astype(F32)
    head = jnp.concatenate([head_ref[...]] * 8, axis=0)
    spread_ref[: 2 * rows, :] = dot(normed_silu(current).astype(BF16), head, ((1,), (1,)))
    lane = lax.broadcasted_iota(jnp.int32, (frames, 128), 1) // 16
    latents = []
    for clip, (first, last) in enumerate(spans):
        latent = jnp.zeros((frames, 128), F32)
        for position in range(4):
            values = spread_ref[pl.ds(rows * clip + 4 * ahead + position, frames, stride=4), :]
            latent = jnp.where(lane == position, values, latent)
        latents.append(jnp.where((own >= first) & (own < last), latent, 0.0))
    tokens = jnp.concatenate(latents, axis=0).astype(BF16)
    hidden = dot(tokens[:, :64], embed_ref[...])
    hidden = hidden - jnp.mean(hidden, axis=1, keepdims=True)
    inverse = lax.rsqrt(jnp.mean(hidden * hidden, axis=1, keepdims=True) + norm_eps)
    lane = lax.broadcasted_iota(jnp.int32, tokens.shape, 1)
    packed = tokens.astype(F32)
    for term in range(3):
        high = inverse.astype(BF16).astype(F32)
        packed = jnp.where(lane == 64 + term, high, packed)
        inverse = inverse - high
    packed = packed.astype(BF16)
    near, far = packed[:frames], packed[frames:]
    return jnp.where(half == 0, near, far), jnp.where(half == 0, far, near)


def encoder_spans(group_ref, start_ref, frames_ref):
    wide = lax.axis_index("wide")
    half, place = wide // HALF, lax.rem(wide, HALF)
    return half, [span_of(HALF * clip + place, group_ref, start_ref, frames_ref) for clip in range(2)]


def encoder_kernel(group_ref, start_ref, frames_ref, slab_ref, conv_ref, head_ref, embed_ref, keep_ref, send_ref, spread_ref):
    half, spans = encoder_spans(group_ref, start_ref, frames_ref)
    slab = slab_ref[:, :16, :].astype(F32)
    edge = jnp.zeros((2, 16, slab.shape[2]), F32)
    keep_ref[...], send_ref[...] = encode(
        slab, edge, spans, half, 2 * slab.shape[0] * half, conv_ref, head_ref, embed_ref, spread_ref
    )


def edge_kernel(
    group_ref, start_ref, frames_ref, slab_ref, passed_ref, keep_in, send_in, conv_ref, head_ref, embed_ref, keep_ref, send_ref, spread_ref
):
    half, spans = encoder_spans(group_ref, start_ref, frames_ref)
    slab = slab_ref[:8, :16, :].astype(F32)
    edge = passed_ref[1:].astype(F32)
    keep, send = encode(slab, edge, spans, half, 2 * slab_ref.shape[0] * half, conv_ref, head_ref, embed_ref, spread_ref)
    keep_ref[...] = jnp.concatenate([keep, keep_in[16:, :]], axis=0)
    send_ref[...] = jnp.concatenate([send, send_in[16:, :]], axis=0)


def back_kernel(token_ref, embed_ref, out_ref):
    embed = embed_ref[...]
    hidden = dot(token_ref[:, :64], embed)
    high, low = split(hidden - jnp.mean(hidden, axis=1, keepdims=True))
    out_ref[...] = dot(embed, high, ((1,), (1,))) + dot(embed, low, ((1,), (1,)))


def critic_kernel(
    group_ref,
    start_ref,
    frames_ref,
    t0_ref,
    t1_ref,
    t2_ref,
    t3_ref,
    near_ref,
    other_ref,
    qgain_ref,
    kgain_ref,
    read_ref,
    *refs,
):
    out_refs, fold_ref = refs[:4], refs[4]
    wide = lax.axis_index("wide")
    first, last = span_of(wide, group_ref, start_ref, frames_ref)
    half, place = wide // HALF, lax.rem(wide, HALF)
    width = qgain_ref.shape[1]
    heads = width // HDIM
    channels = near_ref.shape[2]
    for chunk in range(FOLD_ROWS // 8 * 3):
        apart = [lax.rem(place // bit + chunk // bit, 2) for bit in (8, 16, 2, 4, 1)]
        slot = sum(differs * 2**step for step, differs in enumerate(apart[:4]))
        values = jnp.where(apart[4] == 0, near_ref[slot].astype(F32), other_ref[slot].astype(F32))
        row, column = chunk // 3 * 8, chunk % 3 * width
        fold_ref[row : row + 8, column : column + channels] = values[:8]
        fold_ref[row : row + 8, column + channels : column + width] = values[8:, : width - channels]
    blocks = jnp.concatenate([t0_ref[...], t1_ref[...], t2_ref[...], t3_ref[...]], axis=0)
    tokens = blocks[:, :64]
    rows = tokens.shape[0]
    term = lax.broadcasted_iota(jnp.int32, (128, HDIM), 0)
    inverse = dot(blocks, jnp.where((term >= 64) & (term < 67), 1.0, 0.0).astype(BF16))
    frames = rows // 4
    turn = half * (frames // 2)
    frame_down = lax.rem(lax.broadcasted_iota(jnp.int32, (rows, 1), 0) + turn, frames)
    frame_across = lax.rem(lax.broadcasted_iota(jnp.int32, (1, rows), 1) + turn, frames)
    key_bias = jnp.where((frame_down >= first) & (frame_down < last), 0.0, -jnp.inf)
    query_mask = jnp.where((frame_across >= first) & (frame_across < last), 1.0, 0.0)
    root = 1.0 / HDIM**0.5
    total = jnp.zeros((rows, 64), F32)
    for head in range(heads):
        spans = [pl.ds(part * width + head * HDIM, HDIM) for part in range(3)]
        here = pl.ds(head * HDIM, HDIM)
        folds = [fold_ref[:64, span].astype(BF16) for span in spans]
        q, k, v = (
            dot(tokens, fold) * inverse + fold_ref[64:65, span]
            for fold, span in zip(folds, spans, strict=True)
        )
        read = read_ref[:, here]
        qgain, kgain = qgain_ref[:, here], kgain_ref[:, here]
        rq = lax.rsqrt(jnp.mean(q * q, axis=1, keepdims=True) + norm_eps)
        rk = lax.rsqrt(jnp.mean(k * k, axis=1, keepdims=True) + norm_eps)
        qn = (q * rq * qgain).astype(BF16)
        kn = (k * rk * kgain).astype(BF16)
        readout = jnp.sum(v.astype(BF16).astype(F32) * read, axis=1, keepdims=True)
        scores = dot(kn, qn, ((1,), (1,))) + key_bias
        top = jnp.max(scores, axis=0, keepdims=True)
        weights = jnp.exp2((scores - top) * (root * LOG2E))
        share = query_mask / jnp.sum(weights, axis=0, keepdims=True)
        inner = share * jnp.sum(weights * readout, axis=0, keepdims=True)
        probs = weights * share
        column = jnp.sum(probs, axis=1, keepdims=True)
        score_grad = (probs * (readout - inner)).astype(BF16)
        u = qgain * (dot(score_grad, kn, ((0,), (0,))) * root)
        w = kgain * (dot(score_grad, qn) * root)
        query_grad = rq * u - q * (rq * rq * rq) * jnp.mean(q * u, axis=1, keepdims=True)
        key_grad = rk * w - k * (rk * rk * rk) * jnp.mean(k * w, axis=1, keepdims=True)
        value_grad = column * read
        for grad, fold in zip((query_grad, key_grad, value_grad), folds, strict=True):
            total = total + dot(grad.astype(BF16), fold, ((1,), (1,)))
    for index, ref in enumerate(out_refs):
        ref[...] = total[index * frames : (index + 1) * frames].T


def tail_kernel(features, own_ref, h1_ref, h2_ref, h3_ref, token_ref, back_ref, out_ref):
    total = (own_ref[...] + h1_ref[...]) + (h2_ref[...] + h3_ref[...])
    turned = token_ref[...].astype(F32).T
    inverse = turned[64:65] + turned[65:66] + turned[66:67]
    inner = inverse * (jnp.sum(total * turned[:64], axis=0, keepdims=True) / features)
    grad = inverse * (total - (inner * inverse) * back_ref[...])
    half = lax.axis_index("wide") // HALF
    frames = grad.shape[1]
    out_ref[...] = jnp.where(half == 0, grad, pltpu.roll(grad, frames // 2, 1))


VMEM = pl.BlockSpec(memory_space=pltpu.VMEM)
SMEM = pl.BlockSpec(memory_space=pltpu.SMEM)


def call(kernel, scalars, arrays, out_shape, scratch=(), limit=48, space=VMEM):
    return pl.pallas_call(
        kernel,
        in_specs=[SMEM] * len(scalars) + [space] * len(arrays),
        out_specs=jax.tree.map(lambda _: VMEM, out_shape),
        out_shape=out_shape,
        scratch_shapes=list(scratch),
        compiler_params=pltpu.CompilerParams(vmem_limit_bytes=limit * 2**20),
    )(*scalars, *arrays)


def shape(dims, dtype):
    return jax.ShapeDtypeStruct(dims, dtype)


def on_device(
    features,
    clip_start,
    clip_frames,
    clip_group,
    conv_weight,
    head_weight,
    embed_weight,
    modulation_gain,
    modulation_shift,
    query_weight,
    key_weight,
    value_weight,
    query_gain,
    key_gain,
    read_weight,
):
    clips, channels = features.shape[0], features.shape[3]
    width = query_weight.shape[1]
    model = embed_weight.shape[1]
    with jax.named_scope("pack"):
        arrays = (
            features,
            query_weight,
            key_weight,
            value_weight,
            embed_weight,
            modulation_gain,
            modulation_shift,
            clip_group,
        )
        held = [pltpu.VMEM(a.shape, a.dtype) for a in arrays[:-1]] + [pltpu.SMEM((clips,), jnp.int32)]
        outgoing = call(
            pack_kernel,
            (),
            tuple(pltpu.with_memory_space_constraint(a, pltpu.HBM) for a in arrays),
            shape((HALF, 32, channels), BF16),
            (
                pltpu.VMEM((3, FOLD_ROWS, width), F32),
                *held,
                pltpu.SemaphoreType.DMA((len(arrays),)),
                pltpu.SMEM((clips,), jnp.int32),
            ),
            space=pl.BlockSpec(memory_space=pltpu.HBM),
        )
    with jax.named_scope("exchange"):
        slabs = lax.all_to_all(
            outgoing, "wide", split_axis=0, concat_axis=0, tiled=True, axis_index_groups=HALVES
        )
    spans = (clip_group, clip_start, clip_frames)

    def joined(piece, axis, low):
        return [piece] + [swap(piece, axis, low * apart) for apart in (1, 2, 3)]

    pair = (shape((64, 128), BF16), shape((64, 128), BF16))
    weights = (conv_weight, head_weight.T, embed_weight)
    with jax.named_scope("halves"):
        half_sum = jnp.sum(slabs[:, 16:, :].astype(F32), axis=0).astype(BF16)[None]
        passed = swap(jnp.concatenate([half_sum, slabs[HALF - 2 :, :16]], axis=0), "wide", HALF)
    with jax.named_scope("encoder"):
        keep, send = call(encoder_kernel, spans, (slabs, *weights), pair, (pltpu.VMEM((544, 128), F32),))
    passed, keep, send = lax.optimization_barrier((passed, keep, send))
    with jax.named_scope("edge"):
        keep, send = call(
            edge_kernel, spans, (slabs, passed, keep, send, *weights), pair, (pltpu.VMEM((160, 128), F32),)
        )
    with jax.named_scope("halves"):
        mine = (half_sum.astype(F32) + passed[:1].astype(F32)).astype(BF16)
    with jax.named_scope("rounds"):
        mine = jnp.concatenate(joined(mine, "wide", 8), axis=0)
        mine, keep, send = lax.optimization_barrier((mine, keep, send))
        tokens = jnp.concatenate([keep, swap(send, "wide", HALF)], axis=0)
        mine = jnp.concatenate(joined(mine, "wide", 2), axis=0)
        mine, tokens = lax.optimization_barrier((mine, tokens))
        other = swap(mine, "wide", 1)
        blocks = joined(tokens, "seq", 1)
    with jax.named_scope("critic"):
        sums = call(
            critic_kernel,
            spans,
            (*blocks, mine, other, query_gain[None], key_gain[None], read_weight[None]),
            (shape((64, 128), F32),) * 4,
            (pltpu.VMEM((FOLD_ROWS, 3 * width), F32),),
        )
    with jax.named_scope("tail"):
        *sums, own = lax.optimization_barrier((*sums, blocks[0]))
        back = call(back_kernel, (), (own, embed_weight), shape((64, 128), F32))
        result = call(
            functools.partial(tail_kernel, float(model)),
            (),
            (sums[0], *(swap(sums[d], "seq", d) for d in (1, 2, 3)), own, back),
            shape((64, 128), F32),
        )
    return result.T[None]


def solution(mesh):
    return jax.shard_map(
        on_device,
        mesh=mesh,
        in_specs=(
            P(None, "wide", "seq", None),
            P(),
            P(),
            P(),
            P(),
            P(),
            P(),
            P(),
            P(),
            P("wide", "seq"),
            P("wide", "seq"),
            P("wide", "seq"),
            P("seq"),
            P("seq"),
            P("seq"),
        ),
        out_specs=P("wide", None, "seq"),
        check_vma=False,
    )
```

```python
import functools

import jax
import jax.numpy as jnp
from jax import lax
from jax.experimental import pallas as pl
from jax.experimental.pallas import tpu as pltpu
from jax.sharding import PartitionSpec as P

HDIM = 128
norm_eps = 1e-06
LOG2E = 1.4426950408889634
F32 = jnp.float32
BF16 = jnp.bfloat16

HALF = 32
HALVES = [list(range(HALF)), list(range(HALF, 2 * HALF))]
FOLD_ROWS = 72


def dot(a, b, contract=((1,), (0,))):
    return lax.dot_general(a, b, (contract, ((), ())), preferred_element_type=F32)


def split(values):
    high = values.astype(BF16)
    return high, (values - high.astype(F32)).astype(BF16)


def swap(block, axis, bit):
    size = lax.axis_size(axis)
    return lax.ppermute(block, axis, [(place, place ^ bit) for place in range(size)])


def pack_kernel(*refs):
    arrays, out_ref, held, sem, owner_ref = refs[:5], refs[5], refs[6:11], refs[11], refs[12]
    copies = [pltpu.make_async_copy(a, h, sem.at[i]) for i, (a, h) in enumerate(zip(arrays, held, strict=True))]
    for copy in copies:
        copy.start()
    feat_ref, *weights, group_ref = held
    for copy in copies:
        copy.wait()
    for clip in range(group_ref.shape[0]):
        owner_ref[group_ref[clip]] = jnp.int32(clip)
    channels = feat_ref.shape[3]
    rows, width = weights[0].shape
    low = lax.broadcasted_iota(jnp.int32, (8, 128), 1) < 64
    for place in range(HALF):
        column = min(place, 3 * width // 64 - 1) * 64
        tile = column % width // 128 * 128
        block = weights[column // width][:, tile : tile + 128].astype(F32)
        turned = pltpu.roll(block, 64, 1)
        even, odd = (block, turned) if column % 128 == 0 else (turned, block)
        lanes = []
        for at in range(0, channels * 8 // 64, 16):
            second = odd[at + 8 : at + 16] if at + 8 < rows else jnp.zeros((8, 128), F32)
            lanes.append(jnp.where(low, even[at : at + 8], second))
        near = feat_ref[owner_ref[place]].astype(F32)
        far = feat_ref[owner_ref[HALF + place]].astype(F32)
        slab = jnp.concatenate([near[0], near[1], far[0], far[1], jnp.concatenate(lanes, axis=1)], axis=0)
        out_ref[place] = slab.astype(BF16)


def fold_kernel(slab_ref, embed_ref, gain_ref, shift_ref, out_ref, weight_ref):
    places, channels = slab_ref.shape[0], slab_ref.shape[2]
    slab = slab_ref[...].astype(F32)
    rows = weight_ref.shape[1]
    for at in range(0, rows, 8):
        tile = at // 16 * 128
        piece = slab[:, 16:24, tile : tile + 128].reshape(places * 8, 128)
        if at % 16:
            piece = pltpu.roll(piece, 64, 1)
        weight_ref[:, at : at + 8, :] = piece.reshape(places, 8, 128)
    inner = places * rows
    start = pl.multiple_of(lax.axis_index("wide") // HALF * inner, 128)
    window = pl.ds(start, inner)
    mean = jnp.mean(embed_ref[...].astype(F32), axis=1, keepdims=True)
    scaled = (embed_ref[:, window].astype(F32) - mean) * gain_ref[window][None]
    high, low = split(jnp.concatenate([scaled, shift_ref[window][None], jnp.zeros((7, inner), F32)], axis=0))
    weight = weight_ref[...].reshape(inner, 128).astype(BF16)
    part = dot(high, weight) + dot(low, weight)
    left = lax.broadcasted_iota(jnp.int32, (40, 128), 1) < 64
    packed = jnp.where(left, part[:40], pltpu.roll(part[32:72], 64, 1))
    tiles = [packed[at : at + 8] for at in range(0, 40, 8)] + [jnp.zeros((8, 128), F32)]
    chunk = [jnp.concatenate(tiles[at : at + 3], axis=1) for at in (0, 3)]
    out_ref[0] = jnp.concatenate(chunk, axis=0).astype(BF16)
    out_ref[1] = slab[places - 2, :16].astype(BF16)
    out_ref[2] = slab[places - 1, :16].astype(BF16)


def normed_silu(values):
    factor = lax.rsqrt(jnp.mean(values * values, axis=-1, keepdims=True) + norm_eps)
    scaled = values * factor
    return scaled * (1.0 / (1.0 + jnp.exp(-scaled)))


def span_of(group, group_ref, start_ref, frames_ref):
    clip = jnp.int32(0)
    for index in range(group_ref.shape[0]):
        clip = jnp.where(group_ref[index] == group, jnp.int32(index), clip)
    first = start_ref[clip]
    return first, first + frames_ref[clip]


def encode(slab, edge, spans, half, start, conv_ref, head_ref, embed_ref, spread_ref):
    channels = slab.shape[2]
    frames = slab.shape[0] * 2
    ahead = edge.shape[0] * 2
    rows = 4 * (frames + ahead)
    frame = start - ahead + lax.broadcasted_iota(jnp.int32, (rows, 1), 0) // 4
    own = start + lax.broadcasted_iota(jnp.int32, (frames, 1), 0)
    states = []
    for clip, (first, last) in enumerate(spans):
        here = slice(8 * clip, 8 * clip + 8)
        state = jnp.concatenate(
            [edge[:, here].reshape(4 * ahead, channels), slab[:, here].reshape(4 * frames, channels)], axis=0
        )
        states.append(jnp.where((frame >= jnp.maximum(first, 0)) & (frame < last), state, 0.0))
    current = jnp.concatenate(states, axis=0)
    for layer in range(conv_ref.shape[0]):
        active = normed_silu(current).astype(BF16)
        update = dot(active, conv_ref[layer, 0])
        for tap in range(1, conv_ref.shape[1]):
            update = update + pltpu.roll(dot(active, conv_ref[layer, tap]), 4 * tap, 0)
        current = (current + update).astype(BF16).astype(F32)
    head = jnp.concatenate([head_ref[...]] * 8, axis=0)
    spread_ref[: 2 * rows, :] = dot(normed_silu(current).astype(BF16), head, ((1,), (1,)))
    lane = lax.broadcasted_iota(jnp.int32, (frames, 128), 1) // 16
    latents = []
    for clip, (first, last) in enumerate(spans):
        latent = jnp.zeros((frames, 128), F32)
        for position in range(4):
            values = spread_ref[pl.ds(rows * clip + 4 * ahead + position, frames, stride=4), :]
            latent = jnp.where(lane == position, values, latent)
        latents.append(jnp.where((own >= first) & (own < last), latent, 0.0))
    tokens = jnp.concatenate(latents, axis=0).astype(BF16)
    hidden = dot(tokens[:, :64], embed_ref[...])
    hidden = hidden - jnp.mean(hidden, axis=1, keepdims=True)
    inverse = lax.rsqrt(jnp.mean(hidden * hidden, axis=1, keepdims=True) + norm_eps)
    lane = lax.broadcasted_iota(jnp.int32, tokens.shape, 1)
    packed = tokens.astype(F32)
    for term in range(3):
        high = inverse.astype(BF16).astype(F32)
        packed = jnp.where(lane == 64 + term, high, packed)
        inverse = inverse - high
    packed = packed.astype(BF16)
    near, far = packed[:frames], packed[frames:]
    return jnp.where(half == 0, near, far), jnp.where(half == 0, far, near)


def encoder_spans(group_ref, start_ref, frames_ref):
    wide = lax.axis_index("wide")
    half, place = wide // HALF, lax.rem(wide, HALF)
    return half, [span_of(HALF * clip + place, group_ref, start_ref, frames_ref) for clip in range(2)]


def encoder_kernel(group_ref, start_ref, frames_ref, slab_ref, conv_ref, head_ref, embed_ref, keep_ref, send_ref, spread_ref):
    half, spans = encoder_spans(group_ref, start_ref, frames_ref)
    slab = slab_ref[:, :16, :].astype(F32)
    edge = jnp.zeros((2, 16, slab.shape[2]), F32)
    keep_ref[...], send_ref[...] = encode(
        slab, edge, spans, half, 2 * slab.shape[0] * half, conv_ref, head_ref, embed_ref, spread_ref
    )


def edge_kernel(
    group_ref, start_ref, frames_ref, slab_ref, passed_ref, keep_in, send_in, conv_ref, head_ref, embed_ref, keep_ref, send_ref, spread_ref
):
    half, spans = encoder_spans(group_ref, start_ref, frames_ref)
    slab = slab_ref[:8, :16, :].astype(F32)
    edge = passed_ref[1:].astype(F32)
    keep, send = encode(slab, edge, spans, half, 2 * slab_ref.shape[0] * half, conv_ref, head_ref, embed_ref, spread_ref)
    keep_ref[...] = jnp.concatenate([keep, keep_in[16:, :]], axis=0)
    send_ref[...] = jnp.concatenate([send, send_in[16:, :]], axis=0)


def back_kernel(token_ref, embed_ref, out_ref):
    embed = embed_ref[...]
    hidden = dot(token_ref[:, :64], embed)
    high, low = split(hidden - jnp.mean(hidden, axis=1, keepdims=True))
    out_ref[...] = dot(embed, high, ((1,), (1,))) + dot(embed, low, ((1,), (1,)))


def critic_kernel(
    group_ref,
    start_ref,
    frames_ref,
    t0_ref,
    t1_ref,
    t2_ref,
    t3_ref,
    near_ref,
    other_ref,
    qgain_ref,
    kgain_ref,
    read_ref,
    *refs,
):
    out_refs, fold_ref = refs[:4], refs[4]
    wide = lax.axis_index("wide")
    first, last = span_of(wide, group_ref, start_ref, frames_ref)
    half, place = wide // HALF, lax.rem(wide, HALF)
    width = qgain_ref.shape[1]
    heads = width // HDIM
    low = lax.broadcasted_iota(jnp.int32, (8, 128), 1) < 64
    core = lax.rem(place, 2)
    for pair in range(3 * width // 128):
        apart = [lax.rem(place // bit + 2 * pair // bit, 2) for bit in (8, 16, 2, 4)]
        slot = sum(differs * 2**step for step, differs in enumerate(apart))
        here, there = near_ref[slot].astype(F32), other_ref[slot].astype(F32)
        even, odd = jnp.where(core == 0, here, there), jnp.where(core == 0, there, here)
        column = slice(128 * pair, 128 * pair + 128)
        for tile in range(5):
            down, across = tile // 3 * 8, tile % 3 * 128
            first_half = even[down : down + 8, across : across + 128]
            second_half = odd[down : down + 8, across : across + 128]
            row = 8 * tile
            fold_ref[row : row + 8, column] = jnp.where(low, first_half, pltpu.roll(second_half, 64, 1))
            if tile:
                fold_ref[row + 32 : row + 40, column] = jnp.where(low, pltpu.roll(first_half, 64, 1), second_half)
    blocks = jnp.concatenate([t0_ref[...], t1_ref[...], t2_ref[...], t3_ref[...]], axis=0)
    tokens = blocks[:, :64]
    rows = tokens.shape[0]
    term = lax.broadcasted_iota(jnp.int32, (128, HDIM), 0)
    inverse = dot(blocks, jnp.where((term >= 64) & (term < 67), 1.0, 0.0).astype(BF16))
    frames = rows // 4
    turn = half * (frames // 2)
    frame_down = lax.rem(lax.broadcasted_iota(jnp.int32, (rows, 1), 0) + turn, frames)
    frame_across = lax.rem(lax.broadcasted_iota(jnp.int32, (1, rows), 1) + turn, frames)
    key_bias = jnp.where((frame_down >= first) & (frame_down < last), 0.0, -jnp.inf)
    query_mask = jnp.where((frame_across >= first) & (frame_across < last), 1.0, 0.0)
    root = 1.0 / HDIM**0.5
    total = jnp.zeros((rows, 64), F32)
    for head in range(heads):
        spans = [pl.ds(part * width + head * HDIM, HDIM) for part in range(3)]
        here = pl.ds(head * HDIM, HDIM)
        folds = [fold_ref[:64, span].astype(BF16) for span in spans]
        q, k, v = (
            dot(tokens, fold) * inverse + fold_ref[64:65, span]
            for fold, span in zip(folds, spans, strict=True)
        )
        read = read_ref[:, here]
        qgain, kgain = qgain_ref[:, here], kgain_ref[:, here]
        rq = lax.rsqrt(jnp.mean(q * q, axis=1, keepdims=True) + norm_eps)
        rk = lax.rsqrt(jnp.mean(k * k, axis=1, keepdims=True) + norm_eps)
        qn = (q * rq * qgain).astype(BF16)
        kn = (k * rk * kgain).astype(BF16)
        readout = jnp.sum(v.astype(BF16).astype(F32) * read, axis=1, keepdims=True)
        scores = dot(kn, qn, ((1,), (1,))) + key_bias
        top = jnp.max(scores, axis=0, keepdims=True)
        weights = jnp.exp2((scores - top) * (root * LOG2E))
        share = query_mask / jnp.sum(weights, axis=0, keepdims=True)
        inner = share * jnp.sum(weights * readout, axis=0, keepdims=True)
        probs = weights * share
        column = jnp.sum(probs, axis=1, keepdims=True)
        score_grad = (probs * (readout - inner)).astype(BF16)
        u = qgain * (dot(score_grad, kn, ((0,), (0,))) * root)
        w = kgain * (dot(score_grad, qn) * root)
        query_grad = rq * u - q * (rq * rq * rq) * jnp.mean(q * u, axis=1, keepdims=True)
        key_grad = rk * w - k * (rk * rk * rk) * jnp.mean(k * w, axis=1, keepdims=True)
        value_grad = column * read
        for grad, fold in zip((query_grad, key_grad, value_grad), folds, strict=True):
            total = total + dot(grad.astype(BF16), fold, ((1,), (1,)))
    for index, ref in enumerate(out_refs):
        ref[...] = total[index * frames : (index + 1) * frames].T


def tail_kernel(features, own_ref, h1_ref, h2_ref, h3_ref, token_ref, back_ref, out_ref):
    total = (own_ref[...] + h1_ref[...]) + (h2_ref[...] + h3_ref[...])
    turned = token_ref[...].astype(F32).T
    inverse = turned[64:65] + turned[65:66] + turned[66:67]
    inner = inverse * (jnp.sum(total * turned[:64], axis=0, keepdims=True) / features)
    grad = inverse * (total - (inner * inverse) * back_ref[...])
    half = lax.axis_index("wide") // HALF
    frames = grad.shape[1]
    out_ref[...] = jnp.where(half == 0, grad, pltpu.roll(grad, frames // 2, 1))


VMEM = pl.BlockSpec(memory_space=pltpu.VMEM)
SMEM = pl.BlockSpec(memory_space=pltpu.SMEM)


def call(kernel, scalars, arrays, out_shape, scratch=(), limit=48, space=VMEM):
    return pl.pallas_call(
        kernel,
        in_specs=[SMEM] * len(scalars) + [space] * len(arrays),
        out_specs=jax.tree.map(lambda _: VMEM, out_shape),
        out_shape=out_shape,
        scratch_shapes=list(scratch),
        compiler_params=pltpu.CompilerParams(vmem_limit_bytes=limit * 2**20),
    )(*scalars, *arrays)


def shape(dims, dtype):
    return jax.ShapeDtypeStruct(dims, dtype)


def on_device(
    features,
    clip_start,
    clip_frames,
    clip_group,
    conv_weight,
    head_weight,
    embed_weight,
    modulation_gain,
    modulation_shift,
    query_weight,
    key_weight,
    value_weight,
    query_gain,
    key_gain,
    read_weight,
):
    clips, channels = features.shape[0], features.shape[3]
    width = query_weight.shape[1]
    model = embed_weight.shape[1]
    with jax.named_scope("pack"):
        arrays = (features, query_weight, key_weight, value_weight, clip_group)
        held = [pltpu.VMEM(a.shape, a.dtype) for a in arrays[:-1]] + [pltpu.SMEM((clips,), jnp.int32)]
        outgoing = call(
            pack_kernel,
            (),
            tuple(pltpu.with_memory_space_constraint(a, pltpu.HBM) for a in arrays),
            shape((HALF, 24, channels), BF16),
            (*held, pltpu.SemaphoreType.DMA((len(arrays),)), pltpu.SMEM((clips,), jnp.int32)),
            space=pl.BlockSpec(memory_space=pltpu.HBM),
        )
    with jax.named_scope("exchange"):
        slabs = lax.all_to_all(
            outgoing, "wide", split_axis=0, concat_axis=0, tiled=True, axis_index_groups=HALVES
        )
    spans = (clip_group, clip_start, clip_frames)

    def joined(piece, axis, low):
        return [piece] + [swap(piece, axis, low * apart) for apart in (1, 2, 3)]

    pair = (shape((64, 128), BF16), shape((64, 128), BF16))
    weights = (conv_weight, head_weight.T, embed_weight)
    with jax.named_scope("halves"):
        half_sum = call(
            fold_kernel,
            (),
            (slabs, embed_weight, modulation_gain, modulation_shift),
            shape((3, 16, channels), BF16),
            (pltpu.VMEM((HALF, query_weight.shape[0], 128), F32),),
        )
        passed = swap(half_sum, "wide", HALF)
    with jax.named_scope("encoder"):
        keep, send = call(encoder_kernel, spans, (slabs, *weights), pair, (pltpu.VMEM((544, 128), F32),))
    passed, keep, send = lax.optimization_barrier((passed, keep, send))
    with jax.named_scope("edge"):
        keep, send = call(
            edge_kernel, spans, (slabs, passed, keep, send, *weights), pair, (pltpu.VMEM((160, 128), F32),)
        )
    with jax.named_scope("halves"):
        mine = (half_sum[:1].astype(F32) + passed[:1].astype(F32)).astype(BF16)
    with jax.named_scope("rounds"):
        mine = jnp.concatenate(joined(mine, "wide", 8), axis=0)
        mine, keep, send = lax.optimization_barrier((mine, keep, send))
        tokens = jnp.concatenate([keep, swap(send, "wide", HALF)], axis=0)
        mine = jnp.concatenate(joined(mine, "wide", 2), axis=0)
        mine, tokens = lax.optimization_barrier((mine, tokens))
        other = swap(mine, "wide", 1)
        blocks = joined(tokens, "seq", 1)
    with jax.named_scope("critic"):
        sums = call(
            critic_kernel,
            spans,
            (*blocks, mine, other, query_gain[None], key_gain[None], read_weight[None]),
            (shape((64, 128), F32),) * 4,
            (pltpu.VMEM((FOLD_ROWS, 3 * width), F32),),
        )
    with jax.named_scope("tail"):
        *sums, own = lax.optimization_barrier((*sums, blocks[0]))
        back = call(back_kernel, (), (own, embed_weight), shape((64, 128), F32))
        result = call(
            functools.partial(tail_kernel, float(model)),
            (),
            (sums[0], *(swap(sums[d], "seq", d) for d in (1, 2, 3)), own, back),
            shape((64, 128), F32),
        )
    return result.T[None]


def solution(mesh):
    return jax.shard_map(
        on_device,
        mesh=mesh,
        in_specs=(
            P(None, "wide", "seq", None),
            P(),
            P(),
            P(),
            P(),
            P(),
            P(),
            P(),
            P(),
            P("wide", "seq"),
            P("wide", "seq"),
            P("wide", "seq"),
            P("seq"),
            P("seq"),
            P("seq"),
        ),
        out_specs=P("wide", None, "seq"),
        check_vma=False,
    )
```

```python
import functools

import jax
import jax.numpy as jnp
from jax import lax
from jax.experimental import pallas as pl
from jax.experimental.pallas import tpu as pltpu
from jax.sharding import PartitionSpec as P

HDIM = 128
norm_eps = 1e-06
LOG2E = 1.4426950408889634
F32 = jnp.float32
BF16 = jnp.bfloat16

HALF = 32
HALVES = [list(range(HALF)), list(range(HALF, 2 * HALF))]
FOLD_ROWS = 72


def dot(a, b, contract=((1,), (0,))):
    return lax.dot_general(a, b, (contract, ((), ())), preferred_element_type=F32)


def split(values):
    high = values.astype(BF16)
    return high, (values - high.astype(F32)).astype(BF16)


def swap(block, axis, bit):
    size = lax.axis_size(axis)
    return lax.ppermute(block, axis, [(place, place ^ bit) for place in range(size)])


def pack_kernel(*refs):
    arrays, out_ref, held, sem, owner_ref = refs[:5], refs[5], refs[6:11], refs[11], refs[12]
    copies = [pltpu.make_async_copy(a, h, sem.at[i]) for i, (a, h) in enumerate(zip(arrays, held, strict=True))]
    for copy in copies:
        copy.start()
    feat_ref, *weights, group_ref = held
    for copy in copies:
        copy.wait()
    for clip in range(group_ref.shape[0]):
        owner_ref[group_ref[clip]] = jnp.int32(clip)
    channels = feat_ref.shape[3]
    rows, width = weights[0].shape
    low = lax.broadcasted_iota(jnp.int32, (8, 128), 1) < 64
    for place in range(HALF):
        column = min(place, 3 * width // 64 - 1) * 64
        tile = column % width // 128 * 128
        block = weights[column // width][:, tile : tile + 128].astype(F32)
        turned = pltpu.roll(block, 64, 1)
        even, odd = (block, turned) if column % 128 == 0 else (turned, block)
        lanes = []
        for at in range(0, channels * 8 // 64, 16):
            second = odd[at + 8 : at + 16] if at + 8 < rows else jnp.zeros((8, 128), F32)
            lanes.append(jnp.where(low, even[at : at + 8], second))
        near = feat_ref[owner_ref[place]].astype(F32)
        far = feat_ref[owner_ref[HALF + place]].astype(F32)
        slab = jnp.concatenate([near[0], near[1], far[0], far[1], jnp.concatenate(lanes, axis=1)], axis=0)
        out_ref[place] = slab.astype(BF16)


def fold_kernel(slab_ref, embed_ref, gain_ref, shift_ref, out_ref, weight_ref):
    places, channels = slab_ref.shape[0], slab_ref.shape[2]
    slab = slab_ref[...].astype(F32)
    rows = weight_ref.shape[1]
    for at in range(0, rows, 8):
        tile = at // 16 * 128
        piece = slab[:, 16:24, tile : tile + 128].reshape(places * 8, 128)
        if at % 16:
            piece = pltpu.roll(piece, 64, 1)
        weight_ref[:, at : at + 8, :] = piece.reshape(places, 8, 128)
    inner = places * rows
    start = pl.multiple_of(lax.axis_index("wide") // HALF * inner, 128)
    window = pl.ds(start, inner)
    mean = jnp.mean(embed_ref[...].astype(F32), axis=1, keepdims=True)
    scaled = (embed_ref[:, window].astype(F32) - mean) * gain_ref[window][None]
    high, low = split(jnp.concatenate([scaled, shift_ref[window][None], jnp.zeros((7, inner), F32)], axis=0))
    weight = weight_ref[...].reshape(inner, 128).astype(BF16)
    part = dot(high, weight) + dot(low, weight)
    left = lax.broadcasted_iota(jnp.int32, (40, 128), 1) < 64
    packed = jnp.where(left, part[:40], pltpu.roll(part[32:72], 64, 1))
    tiles = [packed[at : at + 8] for at in range(0, 40, 8)] + [jnp.zeros((8, 128), F32)]
    chunk = [jnp.concatenate(tiles[at : at + 3], axis=1) for at in (0, 3)]
    out_ref[0] = jnp.concatenate(chunk, axis=0).astype(BF16)
    out_ref[1] = slab[places - 2, :16].astype(BF16)
    out_ref[2] = slab[places - 1, :16].astype(BF16)


def normed_silu(values):
    factor = lax.rsqrt(jnp.mean(values * values, axis=-1, keepdims=True) + norm_eps)
    scaled = values * factor
    return scaled * (1.0 / (1.0 + jnp.exp(-scaled)))


def span_of(group, group_ref, start_ref, frames_ref):
    clip = jnp.int32(0)
    for index in range(group_ref.shape[0]):
        clip = jnp.where(group_ref[index] == group, jnp.int32(index), clip)
    first = start_ref[clip]
    return first, first + frames_ref[clip]


def encode(slab, edge, spans, half, start, conv_ref, head_ref, embed_ref, spread_ref):
    channels = slab.shape[2]
    frames = slab.shape[0] * 2
    ahead = edge.shape[0] * 2
    rows = 4 * (frames + ahead)
    frame = start - ahead + lax.broadcasted_iota(jnp.int32, (rows, 1), 0) // 4
    own = start + lax.broadcasted_iota(jnp.int32, (frames, 1), 0)
    states = []
    for clip, (first, last) in enumerate(spans):
        here = slice(8 * clip, 8 * clip + 8)
        state = jnp.concatenate(
            [edge[:, here].reshape(4 * ahead, channels), slab[:, here].reshape(4 * frames, channels)], axis=0
        )
        states.append(jnp.where((frame >= jnp.maximum(first, 0)) & (frame < last), state, 0.0))
    current = jnp.concatenate(states, axis=0)
    for layer in range(conv_ref.shape[0]):
        active = normed_silu(current).astype(BF16)
        update = dot(active, conv_ref[layer, 0])
        for tap in range(1, conv_ref.shape[1]):
            update = update + pltpu.roll(dot(active, conv_ref[layer, tap]), 4 * tap, 0)
        current = (current + update).astype(BF16).astype(F32)
    head = jnp.concatenate([head_ref[...]] * 8, axis=0)
    spread_ref[: 2 * rows, :] = dot(normed_silu(current).astype(BF16), head, ((1,), (1,)))
    lane = lax.broadcasted_iota(jnp.int32, (frames, 128), 1) // 16
    latents = []
    for clip, (first, last) in enumerate(spans):
        latent = jnp.zeros((frames, 128), F32)
        for position in range(4):
            values = spread_ref[pl.ds(rows * clip + 4 * ahead + position, frames, stride=4), :]
            latent = jnp.where(lane == position, values, latent)
        latents.append(jnp.where((own >= first) & (own < last), latent, 0.0))
    tokens = jnp.concatenate(latents, axis=0).astype(BF16)
    hidden = dot(tokens[:, :64], embed_ref[...])
    hidden = hidden - jnp.mean(hidden, axis=1, keepdims=True)
    inverse = lax.rsqrt(jnp.mean(hidden * hidden, axis=1, keepdims=True) + norm_eps)
    lane = lax.broadcasted_iota(jnp.int32, tokens.shape, 1)
    packed = tokens.astype(F32)
    for term in range(3):
        high = inverse.astype(BF16).astype(F32)
        packed = jnp.where(lane == 64 + term, high, packed)
        inverse = inverse - high
    packed = packed.astype(BF16)
    near, far = packed[:frames], packed[frames:]
    return jnp.where(half == 0, near, far), jnp.where(half == 0, far, near)


def encoder_spans(group_ref, start_ref, frames_ref):
    wide = lax.axis_index("wide")
    half, place = wide // HALF, lax.rem(wide, HALF)
    return half, [span_of(HALF * clip + place, group_ref, start_ref, frames_ref) for clip in range(2)]


def encoder_kernel(group_ref, start_ref, frames_ref, slab_ref, conv_ref, head_ref, embed_ref, keep_ref, send_ref, spread_ref):
    half, spans = encoder_spans(group_ref, start_ref, frames_ref)
    slab = slab_ref[:, :16, :].astype(F32)
    edge = jnp.zeros((2, 16, slab.shape[2]), F32)
    keep_ref[...], send_ref[...] = encode(
        slab, edge, spans, half, 2 * slab.shape[0] * half, conv_ref, head_ref, embed_ref, spread_ref
    )


def edge_kernel(
    group_ref, start_ref, frames_ref, slab_ref, passed_ref, keep_in, send_in, conv_ref, head_ref, embed_ref, keep_ref, send_ref, spread_ref
):
    half, spans = encoder_spans(group_ref, start_ref, frames_ref)
    slab = slab_ref[:8, :16, :].astype(F32)
    edge = passed_ref[1:].astype(F32)
    keep, send = encode(slab, edge, spans, half, 2 * slab_ref.shape[0] * half, conv_ref, head_ref, embed_ref, spread_ref)
    keep_ref[...] = jnp.concatenate([keep, keep_in[16:, :]], axis=0)
    send_ref[...] = jnp.concatenate([send, send_in[16:, :]], axis=0)


def back_kernel(token_ref, embed_ref, out_ref):
    embed = embed_ref[...]
    hidden = dot(token_ref[:, :64], embed)
    high, low = split(hidden - jnp.mean(hidden, axis=1, keepdims=True))
    out_ref[...] = dot(embed, high, ((1,), (1,))) + dot(embed, low, ((1,), (1,)))


def critic_kernel(
    group_ref,
    start_ref,
    frames_ref,
    t0_ref,
    t1_ref,
    t2_ref,
    t3_ref,
    y0_ref,
    y1_ref,
    y2_ref,
    y3_ref,
    qgain_ref,
    kgain_ref,
    read_ref,
    *refs,
):
    out_refs, fold_ref = refs[:4], refs[4]
    piece_refs = (y0_ref, y1_ref, y2_ref, y3_ref)
    wide = lax.axis_index("wide")
    first, last = span_of(wide, group_ref, start_ref, frames_ref)
    half, place = wide // HALF, lax.rem(wide, HALF)
    width = qgain_ref.shape[1]
    heads = width // HDIM
    low = lax.broadcasted_iota(jnp.int32, (8, 128), 1) < 64
    core = lax.rem(place, 2)

    def pick(away, slot):
        values = [ref[slot].astype(F32) for ref in piece_refs]
        return jnp.where(
            away < 2, jnp.where(away == 0, values[0], values[1]), jnp.where(away == 2, values[2], values[3])
        )

    for pair in range(3 * width // 128):
        x_low, x_high, y_low, y_high = (lax.rem(place // bit + 2 * pair // bit, 2) for bit in (8, 16, 2, 4))
        slot = lax.rem(x_low + x_high, 2) + 4 * x_high
        away = y_low + 2 * y_high
        even, odd = (pick(away, slot + 2 * side) for side in (core, 1 - core))
        column = slice(128 * pair, 128 * pair + 128)
        for tile in range(5):
            down, across = tile // 3 * 8, tile % 3 * 128
            first_half = even[down : down + 8, across : across + 128]
            second_half = odd[down : down + 8, across : across + 128]
            row = 8 * tile
            fold_ref[row : row + 8, column] = jnp.where(low, first_half, pltpu.roll(second_half, 64, 1))
            if tile:
                fold_ref[row + 32 : row + 40, column] = jnp.where(low, pltpu.roll(first_half, 64, 1), second_half)
    blocks = jnp.concatenate([t0_ref[...], t1_ref[...], t2_ref[...], t3_ref[...]], axis=0)
    tokens = blocks[:, :64]
    rows = tokens.shape[0]
    term = lax.broadcasted_iota(jnp.int32, (128, HDIM), 0)
    inverse = dot(blocks, jnp.where((term >= 64) & (term < 67), 1.0, 0.0).astype(BF16))
    frames = rows // 4
    turn = half * (frames // 2)
    frame_down = lax.rem(lax.broadcasted_iota(jnp.int32, (rows, 1), 0) + turn, frames)
    frame_across = lax.rem(lax.broadcasted_iota(jnp.int32, (1, rows), 1) + turn, frames)
    key_bias = jnp.where((frame_down >= first) & (frame_down < last), 0.0, -jnp.inf)
    query_mask = jnp.where((frame_across >= first) & (frame_across < last), 1.0, 0.0)
    root = 1.0 / HDIM**0.5
    total = jnp.zeros((rows, 64), F32)
    lane = lax.broadcasted_iota(jnp.int32, (1, HDIM), 1)
    value_side = jnp.zeros((FOLD_ROWS, HDIM), F32)
    for head in range(heads):
        span = pl.ds(2 * width + head * HDIM, HDIM)
        reads = jnp.sum(fold_ref[:, span] * read_ref[:, pl.ds(head * HDIM, HDIM)], axis=1, keepdims=True)
        value_side = jnp.where(lane == head, reads, value_side)
    high, low = split(value_side[:64])
    readouts = (dot(tokens, high) + dot(tokens, low)) * inverse + value_side[64:65]
    value_rows = value_side.T
    for head in range(heads):
        spans = [pl.ds(part * width + head * HDIM, HDIM) for part in range(2)]
        here = pl.ds(head * HDIM, HDIM)
        folds = [fold_ref[:64, span].astype(BF16) for span in spans]
        q, k = (
            dot(tokens, fold) * inverse + fold_ref[64:65, span]
            for fold, span in zip(folds, spans, strict=True)
        )
        qgain, kgain = qgain_ref[:, here], kgain_ref[:, here]
        rq = lax.rsqrt(jnp.mean(q * q, axis=1, keepdims=True) + norm_eps)
        rk = lax.rsqrt(jnp.mean(k * k, axis=1, keepdims=True) + norm_eps)
        qn = (q * rq * qgain).astype(BF16)
        kn = (k * rk * kgain).astype(BF16)
        readout = readouts[:, head : head + 1]
        scores = dot(kn, qn, ((1,), (1,))) + key_bias
        top = jnp.max(scores, axis=0, keepdims=True)
        weights = jnp.exp2((scores - top) * (root * LOG2E))
        share = query_mask / jnp.sum(weights, axis=0, keepdims=True)
        inner = share * jnp.sum(weights * readout, axis=0, keepdims=True)
        probs = weights * share
        column = jnp.sum(probs, axis=1, keepdims=True)
        score_grad = (probs * (readout - inner)).astype(BF16)
        u = qgain * (dot(score_grad, kn, ((0,), (0,))) * root)
        w = kgain * (dot(score_grad, qn) * root)
        query_grad = rq * u - q * (rq * rq * rq) * jnp.mean(q * u, axis=1, keepdims=True)
        key_grad = rk * w - k * (rk * rk * rk) * jnp.mean(k * w, axis=1, keepdims=True)
        for grad, fold in zip((query_grad, key_grad), folds, strict=True):
            total = total + dot(grad.astype(BF16), fold, ((1,), (1,)))
        total = total + column * value_rows[head : head + 1, :64]
    for index, ref in enumerate(out_refs):
        ref[...] = total[index * frames : (index + 1) * frames].T


def tail_kernel(features, own_ref, h1_ref, h2_ref, h3_ref, token_ref, back_ref, out_ref):
    total = (own_ref[...] + h1_ref[...]) + (h2_ref[...] + h3_ref[...])
    turned = token_ref[...].astype(F32).T
    inverse = turned[64:65] + turned[65:66] + turned[66:67]
    inner = inverse * (jnp.sum(total * turned[:64], axis=0, keepdims=True) / features)
    grad = inverse * (total - (inner * inverse) * back_ref[...])
    half = lax.axis_index("wide") // HALF
    frames = grad.shape[1]
    out_ref[...] = jnp.where(half == 0, grad, pltpu.roll(grad, frames // 2, 1))


VMEM = pl.BlockSpec(memory_space=pltpu.VMEM)
SMEM = pl.BlockSpec(memory_space=pltpu.SMEM)


def call(kernel, scalars, arrays, out_shape, scratch=(), limit=48, space=VMEM):
    return pl.pallas_call(
        kernel,
        in_specs=[SMEM] * len(scalars) + [space] * len(arrays),
        out_specs=jax.tree.map(lambda _: VMEM, out_shape),
        out_shape=out_shape,
        scratch_shapes=list(scratch),
        compiler_params=pltpu.CompilerParams(vmem_limit_bytes=limit * 2**20),
    )(*scalars, *arrays)


def shape(dims, dtype):
    return jax.ShapeDtypeStruct(dims, dtype)


def on_device(
    features,
    clip_start,
    clip_frames,
    clip_group,
    conv_weight,
    head_weight,
    embed_weight,
    modulation_gain,
    modulation_shift,
    query_weight,
    key_weight,
    value_weight,
    query_gain,
    key_gain,
    read_weight,
):
    clips, channels = features.shape[0], features.shape[3]
    width = query_weight.shape[1]
    model = embed_weight.shape[1]
    with jax.named_scope("pack"):
        arrays = (features, query_weight, key_weight, value_weight, clip_group)
        held = [pltpu.VMEM(a.shape, a.dtype) for a in arrays[:-1]] + [pltpu.SMEM((clips,), jnp.int32)]
        outgoing = call(
            pack_kernel,
            (),
            tuple(pltpu.with_memory_space_constraint(a, pltpu.HBM) for a in arrays),
            shape((HALF, 24, channels), BF16),
            (*held, pltpu.SemaphoreType.DMA((len(arrays),)), pltpu.SMEM((clips,), jnp.int32)),
            space=pl.BlockSpec(memory_space=pltpu.HBM),
        )
    with jax.named_scope("exchange"):
        slabs = lax.all_to_all(
            outgoing, "wide", split_axis=0, concat_axis=0, tiled=True, axis_index_groups=HALVES
        )
    spans = (clip_group, clip_start, clip_frames)

    def joined(piece, bits):
        return jnp.concatenate([piece, swap(piece, "wide", bits)], axis=0)

    pair = (shape((64, 128), BF16), shape((64, 128), BF16))
    weights = (conv_weight, head_weight.T, embed_weight)
    with jax.named_scope("halves"):
        half_sum = call(
            fold_kernel,
            (),
            (slabs, embed_weight, modulation_gain, modulation_shift),
            shape((3, 16, channels), BF16),
            (pltpu.VMEM((HALF, query_weight.shape[0], 128), F32),),
        )
        passed = swap(half_sum, "wide", HALF)
    with jax.named_scope("encoder"):
        keep, send = call(encoder_kernel, spans, (slabs, *weights), pair, (pltpu.VMEM((544, 128), F32),))
    passed, keep, send = lax.optimization_barrier((passed, keep, send))
    with jax.named_scope("edge"):
        keep, send = call(
            edge_kernel, spans, (slabs, passed, keep, send, *weights), pair, (pltpu.VMEM((160, 128), F32),)
        )
    with jax.named_scope("halves"):
        mine = (half_sum[:1].astype(F32) + passed[:1].astype(F32)).astype(BF16)
    with jax.named_scope("rounds"):
        mine = joined(mine, 8)
        mine, keep, send = lax.optimization_barrier((mine, keep, send))
        tokens = jnp.concatenate([keep, swap(send, "wide", HALF)], axis=0)
        mine = joined(mine, 1)
        mine = joined(mine, 24)
        mine, tokens = lax.optimization_barrier((mine, tokens))
        blocks = [tokens] + [swap(tokens, "seq", apart) for apart in (1, 2, 3)]
        pieces = [mine] + [swap(mine, "wide", 2 * apart) for apart in (1, 2, 3)]
    with jax.named_scope("critic"):
        sums = call(
            critic_kernel,
            spans,
            (*blocks, *pieces, query_gain[None], key_gain[None], read_weight[None]),
            (shape((64, 128), F32),) * 4,
            (pltpu.VMEM((FOLD_ROWS, 3 * width), F32),),
        )
    with jax.named_scope("tail"):
        *sums, own = lax.optimization_barrier((*sums, blocks[0]))
        back = call(back_kernel, (), (own, embed_weight), shape((64, 128), F32))
        result = call(
            functools.partial(tail_kernel, float(model)),
            (),
            (sums[0], *(swap(sums[d], "seq", d) for d in (1, 2, 3)), own, back),
            shape((64, 128), F32),
        )
    return result.T[None]


def solution(mesh):
    return jax.shard_map(
        on_device,
        mesh=mesh,
        in_specs=(
            P(None, "wide", "seq", None),
            P(),
            P(),
            P(),
            P(),
            P(),
            P(),
            P(),
            P(),
            P("wide", "seq"),
            P("wide", "seq"),
            P("wide", "seq"),
            P("seq"),
            P("seq"),
            P("seq"),
        ),
        out_specs=P("wide", None, "seq"),
        check_vma=False,
    )
```
